128 devices in a mesh: len: 16 (over z, x), wid: 4 (over y), lay: 2 (over core).
Axes of the slice: x: 4, y: 4, z: 4, core: 2. Of those that a mesh axis runs over, the one named last changes fastest.
Arguments:
- displacement: float32 [3, 64, 32, 256], P(None, 'len', 'wid', 'lay'), may hold values from -0.1 to 0.1
- velocity: float32 [3, 64, 32, 256], P(None, 'len', 'wid', 'lay'), may hold values from -1.5 to 1.5
- lame_first: float32 [64, 32, 256], P('len', 'wid', 'lay'), may hold values from 0.5 to 2
- shear_modulus: float32 [64, 32, 256], P('len', 'wid', 'lay'), may hold values from 0.5 to 2
- nodal_mass: float32 [64, 32, 256], P('len', 'wid', 'lay'), may hold values from 1 to 4
- slave_nodes: int32 [16, 4, 2, 64, 128], P('len', 'wid', 'lay'), may hold values from 0 to 4095
- initial_gap: float32 [16, 4, 2, 64, 128], P('len', 'wid', 'lay'), may hold values from -0.15 to 0.1
- candidate: int32 [16, 4, 2, 64, 128], P('len', 'wid', 'lay'), may hold values from 0 to 127
- pair_owner: int32 [16, 4, 2, 64, 1], P('len', 'wid', 'lay'), may hold values from 0 to 63; in each aligned block of 64 rows (0 to 63, 64 to 127, ..., all dimensions but the last counted through in order) at most 2 rows name the same one
- pair_patch: int32 [16, 4, 2, 64], P('len', 'wid', 'lay'), may hold values from 0 to 31
- master_faces: int32 [16, 4, 2, 32, 128], P('len', 'wid', 'lay'), may hold values from 0 to 2943, as said below
Outputs:
- new_displacement: float32 [3, 64, 32, 256], P(None, 'len', 'wid', 'lay')
- new_velocity: float32 [3, 64, 32, 256], P(None, 'len', 'wid', 'lay')
The draws below stay inside these ranges and needn't reach their ends.
Inputs may be any that keep to these rules, and one draw needn't show every extreme that they name: `slave_nodes`: local node numbers of the device's own block. `candidate`: a face's position within the pair's master patch. `pair_owner`: owners are numbered len index * 4 + wid index and share the device's lay index; among the rows of one device no owner is named more than 2 times, a bound that some block reaches. `pair_patch`: a master patch of the owner. `master_faces`: a face's first node is i * 8 * 128 + j * 128 + k with i < 3 and j < 7, so all 4 of its nodes lie on the owner.
All inputs are finite; a program needn't handle non-finite values.
Results may differ from the reference program's by a relative error of at most 0.00005.
Values sent between devices are 32-bit elements; how exact they have to be, the bound alone decides.
No kernel may reach another device: no remote copies, remote signals or barrier semaphores. Data moves between devices by JAX's collectives and lax.ppermute only.
A program may use at most 64 MiB of HBM per device.

```python
import math
import jax
import jax.numpy as jnp
import numpy as np

CX = 4
CY = 8
CZ = 128
PAIRS = 64
PATCH = 128
MPATCH = 32
STEPS = 2
NX = 64
NY = 32
NZ = 256
CAP = 2
N_LEN = 16
N_WID = 4
N_LAY = 2


def draw_master_faces(key, part):
    shape = (NX // CX, NY // CY, NZ // CZ, MPATCH, PATCH)
    key_x, key_y, key_z = jax.random.split(jax.random.fold_in(key, 17), 3)
    row_x = jax.random.randint(key_x, shape, 0, CX - 1)
    row_y = jax.random.randint(key_y, shape, 0, CY - 1)
    row_z = jax.random.randint(key_z, shape, 0, CZ)
    faces = ((row_x * CY + row_y) * CZ + row_z).astype(jnp.int32)
    highest = ((CX - 2) * CY + CY - 2) * CZ + CZ - 1
    return faces.at[:, :, :, 0, 0].set(highest).astype(jnp.int32)


def set_ends(values, rng, smallest, top_value):
    dims = values.shape
    spot = [jax.random.randint(jax.random.fold_in(rng, axis), (), 0, dims[axis]) for axis in range(len(dims))]
    values = values.at[tuple(spot)].set(smallest)
    longest = dims.index(max(dims))
    spot[longest] = (spot[longest] + 1) % dims[longest]
    return values.at[tuple(spot)].set(top_value)


def levels(stream_key, shape, cuts, least, high):
    gain, own = 1.0, jax.random.fold_in(stream_key, 6)
    for axis_at, blocks in cuts:
        draws = jnp.exp(jax.random.uniform(jax.random.fold_in(own, axis_at), (blocks,), jnp.float32, least / len(cuts), high / len(cuts)))
        gain = gain * jnp.repeat(draws, shape[axis_at] // blocks).reshape([-1 if axis == axis_at else 1 for axis in range(len(shape))])
    return gain


def routed_block(stream_key, own, number, rows, amount, top, reach, skew):
    order = jax.random.permutation(stream_key, amount)
    heavy_load, common = portions_of(amount, rows * top, reach, skew, True), portions_of(amount, rows * top, reach, skew, False)
    places = jnp.arange(amount)

    def named(sizes, offset_by):
        used = int((sizes > 0).sum())
        fixed = max(1, used // 4)
        moved = fixed + (places - fixed + offset_by * (used - fixed)) % max(1, amount - fixed)
        return jnp.zeros((amount,), jnp.int32).at[order[jnp.where(places < fixed, places, moved)]].set(jnp.asarray(sizes, jnp.int32))

    sizes = jnp.where(number % 4 == 0, named(heavy_load, number // 4), named(common, number - number // 4 - 1))
    mixed = jax.random.permutation(jax.random.fold_in(own, 3), amount)
    giver, sink = mixed[0:amount // 2 * 2:2], mixed[1:amount // 2 * 2:2]
    slack = jnp.minimum(sizes[giver] - 1, reach - sizes[sink]) // 2
    slack = jnp.where((giver == order[0]) | (sink == order[0]) | (sizes[sink] == 0), 0, jnp.maximum(slack, 0))
    moved = jax.random.randint(jax.random.fold_in(own, 4), (amount // 2,), 0, 1 << 20) % (slack + 1)
    sizes = sizes.at[giver].add(-moved).at[sink].add(moved)
    items = jnp.searchsorted(jnp.cumsum(sizes), jnp.arange(rows * top), side="right").astype(jnp.int32)
    table = items.reshape(top, rows).T
    table = table[jax.random.permutation(jax.random.fold_in(own, 1), rows)]
    offset_by = jax.random.randint(jax.random.fold_in(own, 2), (rows, 1), 0, top)
    return jnp.take_along_axis(table, (jnp.arange(top)[None, :] + offset_by) % top, axis=1)


def portions_of(number_of, total, reach, skew, full):
    loads = [(1 << 20) // math.isqrt(standing ** skew) + 1 for standing in range(1, number_of + 1)]
    largest = reach if full else min(reach, max(-(-total // number_of), total * loads[0] // sum(loads)))
    least = 1 if total - largest >= number_of - 1 else 0
    given, spare = [largest] + [least] * (number_of - 1), total - largest - least * (number_of - 1)
    while spare > 0:
        candidates = [i for i in range(1, number_of) if given[i] < largest] or [i for i in range(1, number_of) if given[i] < reach]
        mass, budget = sum([loads[i] for i in candidates]), spare
        for i in candidates:
            more = min(reach - given[i], max(1, budget * loads[i] // mass), spare)
            given[i] = given[i] + more
            spare = spare - more
    return np.array(given)


def noise(stream_key, dims, width, reach, pieces=(), kind=jnp.bfloat16):
    loudness = levels(stream_key, dims, pieces, -0.22, 0.18) if pieces else 1.0
    entries = jax.random.normal(stream_key, dims, jnp.float32) * width * loudness
    return jnp.minimum(jnp.maximum(entries, -reach), reach).astype(kind)


def setup_inputs(seed: int = 0) -> dict:
    splits = jax.random.split(jax.random.key(seed), 12)
    displacement = jnp.clip(jax.random.uniform(splits[0], (3, NX, NY, NZ), jnp.float32, -0.1, 0.1) * levels(splits[0], (3, NX, NY, NZ), ((1, 16), (2, 4), (3, 2)), -0.4, 0.0), -0.1, 0.1)
    velocity = noise(splits[1], (3, NX, NY, NZ), 0.3, 1.5, ((1, 16), (2, 4), (3, 2)), jnp.float32)
    lame_first = jnp.clip(jnp.exp(math.log(2.0) - 1.3862944 * jax.random.uniform(splits[2], (NX, NY, NZ), jnp.float32) ** levels(splits[2], (NX, NY, NZ), ((0, 16), (1, 4), (2, 2)), -0.2, 0.2)), 0.5, 2.0)
    shear_modulus = jnp.clip(jnp.exp(math.log(2.0) - 1.3862944 * jax.random.uniform(splits[3], (NX, NY, NZ), jnp.float32) ** levels(splits[3], (NX, NY, NZ), ((0, 16), (1, 4), (2, 2)), -0.2, 0.2)), 0.5, 2.0)
    nodal_mass = jnp.clip(jnp.exp(math.log(4.0) - 1.3862944 * jax.random.uniform(splits[4], (NX, NY, NZ), jnp.float32) ** levels(splits[4], (NX, NY, NZ), ((0, 16), (1, 4), (2, 2)), -0.2, 0.2)), 1.0, 4.0)
    slave_nodes = set_ends(jax.random.randint(splits[5], (N_LEN, N_WID, N_LAY, PAIRS, PATCH), 0, CX * CY * CZ), jax.random.fold_in(splits[5], 1), 0, (CX * CY * CZ) - 1).astype(jnp.int32)
    initial_gap = jnp.clip(-0.15 + 0.25 * jax.random.uniform(splits[6], (N_LEN, N_WID, N_LAY, PAIRS, PATCH), jnp.float32) ** levels(splits[6], (N_LEN, N_WID, N_LAY, PAIRS, PATCH), ((0, 16), (1, 4), (2, 2)), -0.2, 0.2), -0.15, 0.1)
    candidate = set_ends(jax.random.randint(splits[7], (N_LEN, N_WID, N_LAY, PAIRS, PATCH), 0, PATCH), jax.random.fold_in(splits[7], 1), 0, PATCH - 1).astype(jnp.int32)
    pair_owner_keys = jax.random.split(jax.random.fold_in(splits[8], 1), N_LEN * N_WID * N_LAY * PAIRS // PAIRS)
    pair_owner_turns = jax.random.permutation(jax.random.fold_in(splits[8], 3), N_LEN * N_WID * N_LAY * PAIRS // PAIRS)
    pair_owner = jax.vmap(lambda own, number: routed_block(jax.random.fold_in(splits[8], 2), own, number, PAIRS, N_LEN * N_WID, 1, CAP, 2))(pair_owner_keys, pair_owner_turns).reshape((N_LEN, N_WID, N_LAY, PAIRS, 1))
    pair_patch = set_ends(jax.random.randint(splits[9], (N_LEN, N_WID, N_LAY, PAIRS), 0, MPATCH), jax.random.fold_in(splits[9], 1), 0, MPATCH - 1).astype(jnp.int32)
    master_faces = draw_master_faces(jax.random.fold_in(splits[11], 71), 0)
    return {"displacement": displacement, "velocity": velocity, "lame_first": lame_first, "shear_modulus": shear_modulus, "nodal_mass": nodal_mass, "slave_nodes": slave_nodes, "initial_gap": initial_gap, "candidate": candidate, "pair_owner": pair_owner, "pair_patch": pair_patch, "master_faces": master_faces}


penalty = 4.0
hourglass = 0.3
time_step = 0.25
corner_offsets = ((0, 0, 0), (1, 0, 0), (0, 1, 0), (1, 1, 0), (0, 0, 1), (1, 0, 1), (0, 1, 1), (1, 1, 1))

def element_mean(values, counts):
    summed = jnp.zeros(counts, jnp.float32)
    for along_x, along_y, along_z in corner_offsets:
        summed = summed + values[along_x:along_x + counts[0], along_y:along_y + counts[1], along_z:along_z + counts[2]]
    return summed * 0.125

def corner_forces(points, lame_elem, shear_elem, counts):
    corners = []
    for along_x, along_y, along_z in corner_offsets:
        corners.append(points[:, along_x:along_x + counts[0], along_y:along_y + counts[1], along_z:along_z + counts[2]])
    mean_disp = corners[0]
    for corner in corners[1:]:
        mean_disp = mean_disp + corner
    mean_disp = mean_disp * 0.125
    columns = []
    for axis_pos in range(3):
        column = jnp.zeros_like(corners[0])
        for offsets, corner in zip(corner_offsets, corners):
            column = column + (2 * offsets[axis_pos] - 1) * corner
        columns.append(column * 0.25)
    gradient = jnp.stack(columns, axis=1)
    strain_trace = gradient[0, 0] + gradient[1, 1] + gradient[2, 2]
    stress = shear_elem * (gradient + jnp.swapaxes(gradient, 0, 1))
    stress = stress + lame_elem * strain_trace * jnp.eye(3, dtype=jnp.float32)[:, :, None, None, None]
    damping = hourglass * shear_elem
    forces = []
    for offsets, corner in zip(corner_offsets, corners):
        unit_signs = [2 * offsets[0] - 1, 2 * offsets[1] - 1, 2 * offsets[2] - 1]
        traction = unit_signs[0] * stress[:, 0] + unit_signs[1] * stress[:, 1] + unit_signs[2] * stress[:, 2]
        linear = unit_signs[0] * gradient[:, 0] + unit_signs[1] * gradient[:, 1] + unit_signs[2] * gradient[:, 2]
        forces.append(-0.25 * traction - damping * (corner - mean_disp - 0.5 * linear))
    return forces

def face_frame(u_flat, node_one, node_two, node_three, node_four):
    at_one = u_flat[:, node_one]
    at_two = u_flat[:, node_two]
    at_three = u_flat[:, node_three]
    at_four = u_flat[:, node_four]
    centroid = (at_one + at_two + at_three + at_four) * 0.25
    shape_tail = (3,) + (1,) * node_one.ndim
    diag_one = at_three - at_one + jnp.array([1.0, 1.0, 0.0], dtype=jnp.float32).reshape(shape_tail)
    diag_two = at_four - at_two + jnp.array([-1.0, 1.0, 0.0], dtype=jnp.float32).reshape(shape_tail)
    normal = jnp.stack([diag_one[1] * diag_two[2] - diag_one[2] * diag_two[1], diag_one[2] * diag_two[0] - diag_one[0] * diag_two[2], diag_one[0] * diag_two[1] - diag_one[1] * diag_two[0]])
    normal = normal / jnp.sqrt(normal[0] * normal[0] + normal[1] * normal[1] + normal[2] * normal[2])
    return (centroid, normal)

def contact_terms(centroid, normal, slave_disp, gap_start):
    gap_now = gap_start + (slave_disp[0] - centroid[0]) * normal[0] + (slave_disp[1] - centroid[1]) * normal[1] + (slave_disp[2] - centroid[2]) * normal[2]
    penetration = jnp.minimum(gap_now, 0.0)
    return -penalty * penetration * normal

def to_global(local, dev_len, dev_wid, dev_lay):
    index_x = local // (CY * CZ)
    index_y = local // CZ % CY
    index_z = local % CZ
    return ((dev_len * CX + index_x) * NY + (dev_wid * CY + index_y)) * NZ + (dev_lay * CZ + index_z)

def reference(displacement, velocity, lame_first, shear_modulus, nodal_mass, slave_nodes, initial_gap, candidate, pair_owner, pair_patch, master_faces):
    counts = (NX - 1, NY - 1, NZ - 1)
    lame_elem = element_mean(lame_first, counts)
    shear_elem = element_mean(shear_modulus, counts)
    dev_len = jnp.arange(N_LEN, dtype=jnp.int32)[:, None, None, None, None]
    dev_wid = jnp.arange(N_WID, dtype=jnp.int32)[None, :, None, None, None]
    dev_lay = jnp.arange(N_LAY, dtype=jnp.int32)[None, None, :, None, None]
    slaves_global = to_global(slave_nodes, dev_len, dev_wid, dev_lay)
    owners = pair_owner[..., 0]
    own_len = (owners // N_WID)[..., None]
    own_wid = (owners % N_WID)[..., None]
    face_local = master_faces[own_len, own_wid, dev_lay, pair_patch[..., None], candidate]
    node_one = to_global(face_local, own_len, own_wid, dev_lay)
    node_two = node_one + NY * NZ
    node_three = node_one + NY * NZ + NZ
    node_four = node_one + NZ
    for step in range(STEPS):
        forces = corner_forces(displacement, lame_elem, shear_elem, counts)
        internal = jnp.zeros((3, NX, NY, NZ), jnp.float32)
        for offsets, force in zip(corner_offsets, forces):
            padded = jnp.pad(force, ((0, 0), (1, 1), (1, 1), (1, 1)))
            internal = internal + padded[:, 1 - offsets[0]:1 - offsets[0] + NX, 1 - offsets[1]:1 - offsets[1] + NY, 1 - offsets[2]:1 - offsets[2] + NZ]
        u_flat = displacement.reshape(3, -1)
        centroid, normal = face_frame(u_flat, node_one, node_two, node_three, node_four)
        slave_force = contact_terms(centroid, normal, u_flat[:, slaves_global], initial_gap)
        contact = jnp.zeros((3, NX * NY * NZ), jnp.float32).at[:, slaves_global].add(slave_force)
        quarter = -0.25 * slave_force
        contact = contact.at[:, node_one].add(quarter)
        contact = contact.at[:, node_two].add(quarter)
        contact = contact.at[:, node_three].add(quarter)
        contact = contact.at[:, node_four].add(quarter)
        total_force = internal + contact.reshape(3, NX, NY, NZ)
        velocity = velocity + time_step * total_force / nodal_mass[None]
        displacement = displacement + time_step * velocity
    return (displacement, velocity)
```

```python
import jax
import jax.numpy as jnp
from jax import lax
from jax.experimental import pallas as pl
from jax.experimental.pallas import tpu as pltpu
from jax.sharding import PartitionSpec as P

STEPS = 2
PENALTY = 4.0
HOURGLASS = 0.3
TIME_STEP = 0.25

NI, NJ, NK = 4, 8, 128
ROWS = NI * NJ
PAIRS = 64
PATCH = 128
PATCHES = 32
GROUPS = 64
CAP = 2
SLOTS = GROUPS * CAP
F32 = jnp.float32
BF16 = jnp.bfloat16
I32 = jnp.int32


def iota(shape, axis):
    return lax.broadcasted_iota(I32, shape, axis)


def lane_pick(values, index):
    return jnp.take_along_axis(values, index, axis=1, mode="promise_in_bounds")


def parts_3(x):
    high = x.astype(BF16)
    rest = x - high.astype(F32)
    mid = rest.astype(BF16)
    low = (rest - mid.astype(F32)).astype(BF16)
    return high, mid, low


def select_dot(onehot, x):
    high, mid, low = parts_3(x)
    out = jnp.dot(onehot, low, preferred_element_type=F32)
    out = out + jnp.dot(onehot, mid, preferred_element_type=F32)
    return out + jnp.dot(onehot, high, preferred_element_type=F32)


def gather_nodes(u_ref, nodes):
    row = nodes >> 7
    lane = nodes & 127
    out = [jnp.zeros((PAIRS, PATCH), F32) for _ in range(3)]
    for r in range(ROWS):
        here = row == r
        for c in range(3):
            source = jnp.broadcast_to(u_ref[c, r : r + 1, :], (PAIRS, PATCH))
            out[c] = jnp.where(here, lane_pick(source, lane), out[c])
    return out


def up(x, amount):
    return pltpu.roll(x, x.shape[0] - amount, 0)


def patch_table(u_ref, faces):
    frames = []
    one = [u_ref[c] for c in range(3)]
    two = [up(x, 8) for x in one]
    three = [up(x, 9) for x in one]
    four = [up(x, 1) for x in one]
    centroid = [(one[c] + two[c] + three[c] + four[c]) * 0.25 for c in range(3)]
    da = [three[0] - one[0] + 1.0, three[1] - one[1] + 1.0, three[2] - one[2]]
    db = [four[0] - two[0] - 1.0, four[1] - two[1] + 1.0, four[2] - two[2]]
    normal = [
        da[1] * db[2] - da[2] * db[1],
        da[2] * db[0] - da[0] * db[2],
        da[0] * db[1] - da[1] * db[0],
    ]
    length = jnp.sqrt(normal[0] * normal[0] + normal[1] * normal[1] + normal[2] * normal[2])
    normal = [x / length for x in normal]
    offset = centroid[0] * normal[0] + centroid[1] * normal[1] + centroid[2] * normal[2]
    frames = normal + [offset]
    row = faces >> 7
    lane = faces & 127
    out = [jnp.zeros((PATCHES, PATCH), F32) for _ in range(4)]
    for r in range((NI - 1) * NJ):
        if r % NJ == NJ - 1:
            continue
        here = row == r
        for c in range(4):
            source = jnp.broadcast_to(frames[c][r : r + 1, :], (PATCHES, PATCH))
            out[c] = jnp.where(here, lane_pick(source, lane), out[c])
    table = jnp.concatenate(out, axis=1)
    high, mid, low = parts_3(table)
    return jnp.concatenate([high, mid, low, jnp.zeros_like(high)], axis=0)


def scatter_nodes(count, row_lane, forces_ref):
    acc = jnp.zeros((6 * ROWS, PATCH), F32)
    row_at = iota((ROWS, PATCH), 0)
    lane_at = iota((PATCH, PATCH), 0)

    def body(i, acc):
        start = pl.multiple_of(i * 8, 8)
        rows, lanes = row_lane(start)
        parts = [forces_ref[c, pl.ds(start, 8), :] for c in range(6)]
        left = []
        right = []
        for q in range(8):
            here = jnp.broadcast_to(rows[q : q + 1, :], (ROWS, PATCH)) == row_at
            pieces = [
                jnp.where(here, jnp.broadcast_to(part[q : q + 1, :], (ROWS, PATCH)), 0.0)
                for part in parts
            ]
            left.append(jnp.concatenate(pieces, axis=0).astype(BF16))
            chosen = jnp.broadcast_to(lanes[q : q + 1, :], (PATCH, PATCH)) == lane_at
            right.append(jnp.where(chosen, 1.0, 0.0).astype(BF16))
        left = jnp.concatenate(left, axis=1)
        right = jnp.concatenate(right, axis=1)
        return acc + lax.dot_general(
            left, right, (((1,), (1,)), ((), ())), preferred_element_type=F32
        )

    acc = lax.fori_loop(0, count // 8, body, acc)
    return [acc[c * ROWS : (c + 1) * ROWS] + acc[(c + 3) * ROWS : (c + 4) * ROWS] for c in range(3)]


def store_parts(forces_ref, c, start, force):
    high = force.astype(BF16).astype(F32)
    forces_ref[c, start : start + force.shape[0], :] = high
    forces_ref[c + 3, start : start + force.shape[0], :] = force - high


def down_rows(x, amount):
    moved = pltpu.roll(x, amount, 0)
    return jnp.where(iota(x.shape, 0) >= amount, moved, 0.0)


def pair_force(u, normal, offset, gap):
    now = gap + (u[0] * normal[0] + u[1] * normal[1] + u[2] * normal[2]) - offset
    push = -PENALTY * jnp.minimum(now, 0.0)
    return [push * normal[c] for c in range(3)]


def every(ref, start, stride):
    return ref[pl.ds(start, GROUPS, stride=stride), :]


def slabs_kernel(disp, lame, shear, five, low, high):
    for c in range(5):
        block = disp[c] if c < 3 else (lame[...] if c == 3 else shear[...])
        five[c] = block
        low[c] = block[0]
        high[c] = block[NI - 1]


def rim_kernel(block, x_low, x_high, y_low, y_high):
    for c in range(block.shape[0]):
        for out, j in ((y_low, 0), (y_high, NJ - 1)):
            out[c, 0:1, :] = x_low[c, j : j + 1, :]
            for i in range(NI):
                out[c, i + 1 : i + 2, :] = block[c, i, j : j + 1, :]
            out[c, 5:6, :] = x_high[c, j : j + 1, :]
            out[c, 6:8, :] = jnp.zeros((2, NK), F32)


def extend_kernel(block, x_low, x_high, y_low, y_high, out):
    for c in range(block.shape[0]):
        for i in range(NI + 2):
            if i == 0:
                middle = x_low[c]
            elif i == NI + 1:
                middle = x_high[c]
            else:
                middle = block[c, i - 1]
            out[c, i, 1:9, :] = middle
            out[c, i, 0:1, :] = y_low[c, i : i + 1, :]
            out[c, i, 9:10, :] = y_high[c, i : i + 1, :]
            out[c, i, 10:16, :] = jnp.zeros((6, NK), F32)


def far_plane(near, other):
    lay = lax.axis_index("lay")
    lane = iota(near.shape, 2)
    edge = jnp.where(lay == 0, 0, NK - 1)
    shift = jnp.where(lay == 0, NK - 1, 1)
    return pltpu.roll(jnp.where(lane == edge, other, near), shift, 2)


def from_far(x):
    lay = lax.axis_index("lay")
    lane = iota(x.shape, 2)
    edge = jnp.where(lay == 0, 0, NK - 1)
    shift = jnp.where(lay == 0, 1, NK - 1)
    return jnp.where(lane == edge, 0.0, pltpu.roll(x, shift, 2))


def next_row(x):
    return pltpu.roll(x, x.shape[1] - 1, 1)


def element_moduli(near, other):
    total = near + far_plane(near, other)
    total = total + next_row(total)
    total = (total[0:5] + total[1:6]) * 0.125
    plane = iota(total.shape, 0)
    row = iota(total.shape, 1)
    at_len = lax.axis_index("len")
    at_wid = lax.axis_index("wid")
    outside = (plane == 0) & (at_len == 0)
    outside |= (plane == NI) & (at_len == lax.axis_size("len") - 1)
    outside |= (row == 0) & (at_wid == 0)
    outside |= (row == NJ) & (at_wid == lax.axis_size("wid") - 1)
    return jnp.where(outside, 0.0, total)


def internal_force(near_ref, other_ref, lame, shear):
    sigma = jnp.where(lax.axis_index("lay") == 0, 1.0, -1.0)
    grad = []
    means = []
    for c in range(3):
        near = near_ref[c]
        far = far_plane(near, other_ref[c])
        both = far + near
        diff = far - near
        both_next = next_row(both)
        sums = both + both_next
        cross = both_next - both
        tall = diff + next_row(diff)
        means.append((sums[0:5] + sums[1:6]) * 0.125)
        grad.append(
            [
                (sums[1:6] - sums[0:5]) * 0.25,
                (cross[0:5] + cross[1:6]) * 0.25,
                (tall[0:5] + tall[1:6]) * (0.25 * sigma),
            ]
        )
    pressure = lame * (grad[0][0] + grad[1][1] + grad[2][2])
    damping = HOURGLASS * shear
    damp_x = damping[0:4] + damping[1:5]
    damp_y = damp_x + next_row(damp_x)
    damp = (damp_y + from_far(damp_y))[:, 0:8]
    out = []
    for c in range(3):
        flux = []
        for j in range(3):
            stress = shear * (grad[c][j] + grad[j][c])
            if c == j:
                stress = stress + pressure
            flux.append(0.5 * damping * grad[c][j] - 0.25 * stress)
        lead = damping * means[c]
        depth = flux[2] * sigma
        lead_x = (lead[0:4] + lead[1:5]) + (flux[0][0:4] - flux[0][1:5])
        side_x = flux[1][0:4] + flux[1][1:5]
        depth_x = depth[0:4] + depth[1:5]
        lead_y = (lead_x + next_row(lead_x)) + (side_x - next_row(side_x))
        depth_y = depth_x + next_row(depth_x)
        force = (lead_y - depth_y) + from_far(lead_y + depth_y)
        out.append(force[:, 0:8] - near_ref[c, 1:5, 1:9, :] * damp)
    return out


def internal_first_kernel(near, other, out, moduli):
    lame = element_moduli(near[3], other[3])
    shear = element_moduli(near[4], other[4])
    moduli[0] = lame
    moduli[1] = shear
    for c, force in enumerate(internal_force(near, other, lame, shear)):
        out[c] = force


def internal_kernel(near, other, moduli, out):
    for c, force in enumerate(internal_force(near, other, moduli[0], moduli[1])):
        out[c] = force


def column_to_row(column):
    size = column.shape[0]
    eye = iota((size, size), 0) == iota((size, size), 1)
    return jnp.sum(jnp.where(eye, column, 0.0), axis=0, keepdims=True)


def row_to_column(row):
    size = row.shape[1]
    eye = iota((size, size), 0) == iota((size, size), 1)
    return jnp.sum(jnp.where(eye, row, 0.0), axis=1, keepdims=True)


def request_kernel(u, slaves, gaps, chosen, owners, wanted, send, slot_of, at_slaves):
    owner = owners[...].astype(F32)
    owner_row = column_to_row(owner)
    same = (owner == owner_row) & (iota((PAIRS, PAIRS), 1) < iota((PAIRS, PAIRS), 0))
    rank = jnp.max(jnp.where(same, 1.0, 0.0), axis=1, keepdims=True)
    slot = rank * GROUPS + owner
    slot_row = column_to_row(slot)
    slot_of[...] = jnp.where(slot == iota((PAIRS, SLOTS), 1).astype(F32), 1.0, 0.0)
    place = jnp.where(slot_row == iota((SLOTS, PAIRS), 0).astype(F32), 1.0, 0.0).astype(BF16)
    values = gather_nodes(u, slaves[...])
    for c in range(3):
        at_slaves[c] = values[c]
    exact = jnp.concatenate(values + [gaps[...]], axis=1)
    moved = select_dot(place, exact)
    patch = jnp.broadcast_to(row_to_column(wanted[...].astype(F32) + 1.0), (PAIRS, PATCH))
    whole = jnp.concatenate([chosen[...].astype(F32), patch], axis=1).astype(BF16)
    moved_whole = jnp.dot(place, whole, preferred_element_type=F32)
    for t in range(CAP):
        part = slice(t * GROUPS, (t + 1) * GROUPS)
        for c in range(4):
            send[pl.ds(t * 4 + c, GROUPS, stride=16), :] = moved[part, c * 128 : (c + 1) * 128]
        for c in range(2):
            send[pl.ds(8 + t * 2 + c, GROUPS, stride=16), :] = moved_whole[
                part, c * 128 : (c + 1) * 128
            ]
    for c in range(12, 16):
        send[pl.ds(c, GROUPS, stride=16), :] = jnp.zeros((GROUPS, PATCH), F32)


def wanted_rows(arrived):
    patch = jnp.concatenate([every(arrived, 9, 16), every(arrived, 11, 16)], axis=0)
    cand = jnp.concatenate([every(arrived, 8, 16), every(arrived, 10, 16)], axis=0)
    at = (iota((SLOTS, PATCH), 1) % PATCHES + 1).astype(F32)
    onehot = jnp.where(patch == at, 1.0, 0.0).astype(BF16)
    return onehot, cand.astype(I32)


def table_kernel(u, faces, table):
    table[...] = patch_table(u, faces[...])


def reply_kernel(arrived, table, faces, send, face_row, face_lane):
    onehot, cand = wanted_rows(arrived)
    tiles = jnp.dot(onehot, table[...], preferred_element_type=F32)
    for c in range(4):
        picked = lane_pick(tiles[:, c * 128 : (c + 1) * 128], cand)
        for t in range(CAP):
            send[pl.ds(t * 4 + c, GROUPS, stride=8), :] = picked[t * GROUPS : (t + 1) * GROUPS]
    index = jnp.concatenate([faces[...] >> 7, faces[...] & 127], axis=1).astype(F32)
    index = jnp.concatenate(
        [index, jnp.zeros((PATCH - PATCHES, 2 * PATCH), F32)], axis=0
    ).astype(BF16)
    index = jnp.dot(onehot, index, preferred_element_type=F32)
    face_row[...] = lane_pick(index[:, 0:128], cand).astype(I32)
    face_lane[...] = lane_pick(index[:, 128:256], cand).astype(I32)


def owner_forces(values, gap_source, frames, stride, offset, frame_stride, frame_offset, scratch):
    for t in range(CAP):
        u = [every(values, t * offset + c, stride) for c in range(3)]
        gap = every(gap_source, t * 4 + 3, 16)
        frame = [every(frames, t * frame_offset[1] + frame_offset[0] + c, frame_stride) for c in range(4)]
        force = pair_force(u, frame[0:3], frame[3], gap)
        for c in range(3):
            store_parts(scratch, c, t * GROUPS, -0.25 * force[c])


def face_contact(face_row, face_lane, scratch):
    def row_lane(start):
        return face_row[pl.ds(start, 8), :], face_lane[pl.ds(start, 8), :]

    faces = scatter_nodes(SLOTS, row_lane, scratch)
    return [x + down_rows(x, 8) + down_rows(x, 9) + down_rows(x, 1) for x in faces]


def slave_contact(arrived, stride, offset, slot_of, at_slaves, gaps, slaves, scratch):
    onehot = slot_of[...].astype(BF16)
    slots = []
    for c in range(4):
        slots.append(
            jnp.concatenate(
                [every(arrived, t * offset[1] + offset[0] + c, stride) for t in range(CAP)], axis=0
            )
        )
    mine = select_dot(onehot, jnp.concatenate(slots, axis=1))
    frame = [mine[:, c * 128 : (c + 1) * 128] for c in range(4)]
    force = pair_force([at_slaves[c] for c in range(3)], frame[0:3], frame[3], gaps[...])
    for c in range(3):
        store_parts(scratch, c, 0, force[c])

    def row_lane(start):
        nodes = slaves[pl.ds(start, 8), :]
        return nodes >> 7, nodes & 127

    return scatter_nodes(PAIRS, row_lane, scratch)


def reaction_kernel(arrived, frames, face_row, face_lane, out, scratch):
    owner_forces(arrived, arrived, frames, 16, 4, 8, (0, 4), scratch)
    for c, force in enumerate(face_contact(face_row, face_lane, scratch)):
        out[c] = force


def advance(c, force, disp, vel, mass, new_disp, new_vel):
    moved = vel[c] + TIME_STEP * force / mass[...]
    new_vel[c] = moved
    place = disp[c] + TIME_STEP * moved
    new_disp[c] = place
    return place


def middle_kernel(
    arrived, slot_of, at_slaves, gaps, slaves, reaction, internal, disp, vel, mass,
    new_disp, new_vel, low, high, scratch,
):
    contact = slave_contact(arrived, 8, (0, 4), slot_of, at_slaves, gaps, slaves, scratch)
    for c in range(3):
        force = internal[c] + (contact[c] + reaction[c])
        place = advance(c, force, disp, vel, mass, new_disp, new_vel)
        low[c] = place[0:NJ]
        high[c] = place[ROWS - NJ : ROWS]


def second_kernel(u, slaves, faces, slot_of, arrived, send, at_slaves):
    values = gather_nodes(u, slaves[...])
    for c in range(3):
        at_slaves[c] = values[c]
    place = slot_of[...].astype(BF16)
    high, mid, low = parts_3(jnp.concatenate(values, axis=1))
    dims = (((0,), (0,)), ((), ()))
    moved = lax.dot_general(place, low, dims, preferred_element_type=F32)
    moved = moved + lax.dot_general(place, mid, dims, preferred_element_type=F32)
    moved = moved + lax.dot_general(place, high, dims, preferred_element_type=F32)
    table = patch_table(u, faces[...])
    onehot, cand = wanted_rows(arrived)
    tiles = jnp.dot(onehot, table, preferred_element_type=F32)
    for t in range(CAP):
        part = slice(t * GROUPS, (t + 1) * GROUPS)
        for c in range(3):
            send[pl.ds(t * 8 + c, GROUPS, stride=16), :] = moved[part, c * 128 : (c + 1) * 128]
        send[pl.ds(t * 8 + 7, GROUPS, stride=16), :] = jnp.zeros((GROUPS, PATCH), F32)
    for c in range(4):
        picked = lane_pick(tiles[:, c * 128 : (c + 1) * 128], cand)
        for t in range(CAP):
            send[pl.ds(t * 8 + 3 + c, GROUPS, stride=16), :] = picked[
                t * GROUPS : (t + 1) * GROUPS
            ]


def last_kernel(
    arrived, sent, first, face_row, face_lane, slot_of, at_slaves, gaps, slaves, internal,
    disp, vel, mass, new_disp, new_vel, scratch, slave_scratch,
):
    owner_forces(arrived, first, sent, 16, 8, 16, (3, 8), scratch)
    reaction = face_contact(face_row, face_lane, scratch)
    contact = slave_contact(arrived, 16, (3, 8), slot_of, at_slaves, gaps, slaves, slave_scratch)
    for c in range(3):
        force = internal[c] + (contact[c] + reaction[c])
        advance(c, force, disp, vel, mass, new_disp, new_vel)


def f32(*shape):
    return jax.ShapeDtypeStruct(shape, F32)


def i32(*shape):
    return jax.ShapeDtypeStruct(shape, I32)


def call(kernel, outs, *args, scratch=()):
    return pl.pallas_call(
        kernel,
        out_shape=outs,
        scratch_shapes=[pltpu.VMEM(s, F32) for s in scratch],
        name=kernel.__name__,
    )(*args)


def shift_pair(low, high, axis):
    count = lax.axis_size(axis)
    from_low = lax.ppermute(high, axis, [(i, i + 1) for i in range(count - 1)])
    from_high = lax.ppermute(low, axis, [(i + 1, i) for i in range(count - 1)])
    return from_low, from_high


def extended(block, low, high):
    parts = block.shape[0]
    x_low, x_high = shift_pair(low, high, "len")
    low, high = call(rim_kernel, (f32(parts, 8, NK), f32(parts, 8, NK)), block, x_low, x_high)
    y_low, y_high = shift_pair(low, high, "wid")
    near = call(
        extend_kernel, f32(parts, NI + 2, 16, NK), block, x_low, x_high, y_low, y_high
    )
    return near, lax.ppermute(near, "lay", [(0, 1), (1, 0)])


def exchange(buffer):
    chunk = buffer.reshape(GROUPS, -1, PATCH)
    out = lax.all_to_all(chunk, ("len", "wid"), split_axis=0, concat_axis=0, tiled=True)
    return out.reshape(buffer.shape)


def per_device(
    displacement, velocity, lame_first, shear_modulus, nodal_mass, slave_nodes, initial_gap,
    candidate, pair_owner, pair_patch, master_faces,
):
    slaves = slave_nodes.reshape(PAIRS, PATCH)
    gaps = initial_gap.reshape(PAIRS, PATCH)
    chosen = candidate.reshape(PAIRS, PATCH)
    owners = pair_owner.reshape(PAIRS, 1)
    wanted = pair_patch.reshape(1, PAIRS)
    faces = master_faces.reshape(PATCHES, PATCH)
    u = displacement.reshape(3, ROWS, NK)
    v = velocity.reshape(3, ROWS, NK)
    mass = nodal_mass.reshape(ROWS, NK)
    five, low, high = call(
        slabs_kernel,
        (f32(5, NI, NJ, NK), f32(5, NJ, NK), f32(5, NJ, NK)),
        displacement, lame_first, shear_modulus,
    )
    near, other = extended(five, low, high)
    send, slot_of, at_slaves = call(
        request_kernel,
        (f32(GROUPS * 16, PATCH), f32(PAIRS, SLOTS), f32(3, PAIRS, PATCH)),
        u, slaves, gaps, chosen, owners, wanted,
    )
    first = exchange(send)
    table = call(table_kernel, jax.ShapeDtypeStruct((128, 512), BF16), u, faces)
    reply, face_row, face_lane = call(
        reply_kernel,
        (f32(GROUPS * 8, PATCH), i32(SLOTS, PATCH), i32(SLOTS, PATCH)),
        first, table, faces,
    )
    arrived = exchange(reply)
    reaction = call(
        reaction_kernel, f32(3, ROWS, NK), first, reply, face_row, face_lane,
        scratch=[(6, SLOTS, PATCH)],
    )
    internal, moduli = call(
        internal_first_kernel, (f32(3, NI, NJ, NK), f32(2, 5, 16, NK)), near, other
    )
    u, v, low, high = call(
        middle_kernel,
        (f32(3, ROWS, NK), f32(3, ROWS, NK), f32(3, NJ, NK), f32(3, NJ, NK)),
        arrived, slot_of, at_slaves, gaps, slaves, reaction, internal.reshape(3, ROWS, NK),
        u, v, mass,
        scratch=[(6, PAIRS, PATCH)],
    )
    near, other = extended(u.reshape(3, NI, NJ, NK), low, high)
    sent, at_slaves = call(
        second_kernel,
        (f32(GROUPS * 16, PATCH), f32(3, PAIRS, PATCH)),
        u, slaves, faces, slot_of, first,
    )
    arrived = exchange(sent)
    internal = call(internal_kernel, f32(3, NI, NJ, NK), near, other, moduli)
    u, v = call(
        last_kernel,
        (f32(3, ROWS, NK), f32(3, ROWS, NK)),
        arrived, sent, first, face_row, face_lane, slot_of, at_slaves, gaps, slaves,
        internal.reshape(3, ROWS, NK), u, v, mass,
        scratch=[(6, SLOTS, PATCH), (6, PAIRS, PATCH)],
    )
    return u.reshape(displacement.shape), v.reshape(velocity.shape)


def solution(mesh):
    nodal = P("len", "wid", "lay")
    vector = P(None, "len", "wid", "lay")
    in_specs = (
        vector, vector, nodal, nodal, nodal,
        P("len", "wid", "lay", None, None),
        P("len", "wid", "lay", None, None),
        P("len", "wid", "lay", None, None),
        P("len", "wid", "lay", None, None),
        P("len", "wid", "lay", None),
        P("len", "wid", "lay", None, None),
    )
    return jax.shard_map(
        per_device, mesh=mesh, in_specs=in_specs, out_specs=(vector, vector), check_vma=False
    )
```

```python
import jax
import jax.numpy as jnp
from jax import lax
from jax.experimental import pallas as pl
from jax.experimental.pallas import tpu as pltpu
from jax.sharding import PartitionSpec as P


PENALTY = 4.0
HOURGLASS = 0.3
TIME_STEP = 0.25

NI, NJ, NK = 4, 8, 128
ROWS = NI * NJ
PAIRS = 64
PATCH = 128
PATCHES = 32
GROUPS = 64
CAP = 2
SLOTS = GROUPS * CAP
F32 = jnp.float32
BF16 = jnp.bfloat16
I32 = jnp.int32


def iota(shape, axis):
    return lax.broadcasted_iota(I32, shape, axis)


def lane_pick(values, index):
    return jnp.take_along_axis(values, index, axis=1, mode="promise_in_bounds")


def parts_3(x):
    high = x.astype(BF16)
    rest = x - high.astype(F32)
    mid = rest.astype(BF16)
    low = (rest - mid.astype(F32)).astype(BF16)
    return high, mid, low


def select_dot(onehot, x):
    high, mid, low = parts_3(x)
    out = jnp.dot(onehot, low, preferred_element_type=F32)
    out = out + jnp.dot(onehot, mid, preferred_element_type=F32)
    return out + jnp.dot(onehot, high, preferred_element_type=F32)


def gather_nodes(u_ref, nodes):
    row = nodes >> 7
    lane = nodes & 127
    out = [jnp.zeros((PAIRS, PATCH), F32) for _ in range(3)]
    for r in range(ROWS):
        here = row == r
        for c in range(3):
            source = jnp.broadcast_to(u_ref[c, r : r + 1, :], (PAIRS, PATCH))
            out[c] = jnp.where(here, lane_pick(source, lane), out[c])
    return out


def up(x, amount):
    return pltpu.roll(x, x.shape[0] - amount, 0)


def patch_table(u_ref, faces):
    frames = []
    one = [u_ref[c] for c in range(3)]
    two = [up(x, 8) for x in one]
    three = [up(x, 9) for x in one]
    four = [up(x, 1) for x in one]
    centroid = [(one[c] + two[c] + three[c] + four[c]) * 0.25 for c in range(3)]
    da = [three[0] - one[0] + 1.0, three[1] - one[1] + 1.0, three[2] - one[2]]
    db = [four[0] - two[0] - 1.0, four[1] - two[1] + 1.0, four[2] - two[2]]
    normal = [
        da[1] * db[2] - da[2] * db[1],
        da[2] * db[0] - da[0] * db[2],
        da[0] * db[1] - da[1] * db[0],
    ]
    length = jnp.sqrt(normal[0] * normal[0] + normal[1] * normal[1] + normal[2] * normal[2])
    normal = [x / length for x in normal]
    offset = centroid[0] * normal[0] + centroid[1] * normal[1] + centroid[2] * normal[2]
    frames = normal + [offset]
    row = faces >> 7
    lane = faces & 127
    out = [jnp.zeros((PATCHES, PATCH), F32) for _ in range(4)]
    for r in range((NI - 1) * NJ):
        if r % NJ == NJ - 1:
            continue
        here = row == r
        for c in range(4):
            source = jnp.broadcast_to(frames[c][r : r + 1, :], (PATCHES, PATCH))
            out[c] = jnp.where(here, lane_pick(source, lane), out[c])
    table = jnp.concatenate(out, axis=1)
    high, mid, low = parts_3(table)
    return jnp.concatenate([high, mid, low, jnp.zeros_like(high)], axis=0)


def packed_row(x, q):
    return jnp.broadcast_to(x[q : q + 1, :], (16, PATCH)).astype(BF16)


def scatter_nodes(count, row_lane, forces_ref):
    half = ROWS // 2
    row_at = iota((half, PATCH), 0).astype(F32).astype(BF16)
    lane_at = iota((2 * PATCH, PATCH), 0).astype(F32).astype(BF16)
    none = jnp.zeros((half, PATCH), BF16)

    def body(i, acc):
        start = pl.multiple_of(i * 32, 32)
        rows, lanes = row_lane(start)
        lanes = (lanes + (rows >> 4) * PATCH).astype(F32)
        rows = (rows & (half - 1)).astype(F32)
        parts = [forces_ref[c, pl.ds(start, 32), :] for c in range(6)]
        left = []
        right = []
        for q in range(32):
            here = packed_row(rows, q) == row_at
            pieces = [jnp.where(here, packed_row(part, q), none) for part in parts]
            left.append(jnp.concatenate(pieces, axis=0))
            chosen = jnp.concatenate([packed_row(lanes, q)] * 16, axis=0) == lane_at
            right.append(jnp.where(chosen, jnp.ones_like(lane_at), jnp.zeros_like(lane_at)))
        left = jnp.concatenate(left, axis=1)
        right = jnp.concatenate(right, axis=1)
        return acc + lax.dot_general(
            left, right, (((1,), (1,)), ((), ())), preferred_element_type=F32
        )

    acc = lax.fori_loop(0, count // 32, body, jnp.zeros((6 * half, 2 * PATCH), F32))
    acc = acc[0 : 3 * half] + acc[3 * half : 6 * half]
    out = []
    for c in range(3):
        part = acc[c * half : (c + 1) * half]
        out.append(jnp.concatenate([part[:, 0:PATCH], part[:, PATCH:]], axis=0))
    return out


def store_parts(forces_ref, c, start, force):
    high = force.astype(BF16).astype(F32)
    forces_ref[c, start : start + force.shape[0], :] = high
    forces_ref[c + 3, start : start + force.shape[0], :] = force - high


def down_rows(x, amount):
    moved = pltpu.roll(x, amount, 0)
    return jnp.where(iota(x.shape, 0) >= amount, moved, 0.0)


def pair_force(u, normal, offset, gap):
    now = gap + (u[0] * normal[0] + u[1] * normal[1] + u[2] * normal[2]) - offset
    push = -PENALTY * jnp.minimum(now, 0.0)
    return [push * normal[c] for c in range(3)]


def every(ref, start, stride):
    return ref[pl.ds(start, GROUPS, stride=stride), :]


def slabs_kernel(disp, lame, shear, five, low, high):
    for c in range(5):
        block = disp[c] if c < 3 else (lame[...] if c == 3 else shear[...])
        five[c] = block
        low[c] = block[0]
        high[c] = block[NI - 1]


def rim_kernel(block, x_low, x_high, y_low, y_high):
    for c in range(block.shape[0]):
        for out, j in ((y_low, 0), (y_high, NJ - 1)):
            out[c, 0:1, :] = x_low[c, j : j + 1, :]
            for i in range(NI):
                out[c, i + 1 : i + 2, :] = block[c, i, j : j + 1, :]
            out[c, 5:6, :] = x_high[c, j : j + 1, :]
            out[c, 6:8, :] = jnp.zeros((2, NK), F32)


def extend_kernel(block, x_low, x_high, y_low, y_high, out):
    for c in range(block.shape[0]):
        for i in range(NI + 2):
            if i == 0:
                middle = x_low[c]
            elif i == NI + 1:
                middle = x_high[c]
            else:
                middle = block[c, i - 1]
            out[c, i, 1:9, :] = middle
            out[c, i, 0:1, :] = y_low[c, i : i + 1, :]
            out[c, i, 9:10, :] = y_high[c, i : i + 1, :]
            out[c, i, 10:16, :] = jnp.zeros((6, NK), F32)


def far_plane(near, other):
    lay = lax.axis_index("lay")
    lane = iota(near.shape, 2)
    edge = jnp.where(lay == 0, 0, NK - 1)
    shift = jnp.where(lay == 0, NK - 1, 1)
    return pltpu.roll(jnp.where(lane == edge, other, near), shift, 2)


def from_far(x):
    lay = lax.axis_index("lay")
    lane = iota(x.shape, 2)
    edge = jnp.where(lay == 0, 0, NK - 1)
    shift = jnp.where(lay == 0, 1, NK - 1)
    return jnp.where(lane == edge, 0.0, pltpu.roll(x, shift, 2))


def next_row(x):
    return pltpu.roll(x, x.shape[1] - 1, 1)


def element_moduli(near, other):
    total = near + far_plane(near, other)
    total = total + next_row(total)
    total = (total[0:5] + total[1:6]) * 0.125
    plane = iota(total.shape, 0)
    row = iota(total.shape, 1)
    at_len = lax.axis_index("len")
    at_wid = lax.axis_index("wid")
    outside = (plane == 0) & (at_len == 0)
    outside |= (plane == NI) & (at_len == lax.axis_size("len") - 1)
    outside |= (row == 0) & (at_wid == 0)
    outside |= (row == NJ) & (at_wid == lax.axis_size("wid") - 1)
    return jnp.where(outside, 0.0, total)


def internal_force(near_ref, other_ref, lame, shear):
    sigma = jnp.where(lax.axis_index("lay") == 0, 1.0, -1.0)
    grad = []
    means = []
    for c in range(3):
        near = near_ref[c]
        far = far_plane(near, other_ref[c])
        both = far + near
        diff = far - near
        both_next = next_row(both)
        sums = both + both_next
        cross = both_next - both
        tall = diff + next_row(diff)
        means.append((sums[0:5] + sums[1:6]) * 0.125)
        grad.append(
            [
                (sums[1:6] - sums[0:5]) * 0.25,
                (cross[0:5] + cross[1:6]) * 0.25,
                (tall[0:5] + tall[1:6]) * (0.25 * sigma),
            ]
        )
    pressure = lame * (grad[0][0] + grad[1][1] + grad[2][2])
    damping = HOURGLASS * shear
    damp_x = damping[0:4] + damping[1:5]
    damp_y = damp_x + next_row(damp_x)
    damp = (damp_y + from_far(damp_y))[:, 0:8]
    out = []
    for c in range(3):
        flux = []
        for j in range(3):
            stress = shear * (grad[c][j] + grad[j][c])
            if c == j:
                stress = stress + pressure
            flux.append(0.5 * damping * grad[c][j] - 0.25 * stress)
        lead = damping * means[c]
        depth = flux[2] * sigma
        lead_x = (lead[0:4] + lead[1:5]) + (flux[0][0:4] - flux[0][1:5])
        side_x = flux[1][0:4] + flux[1][1:5]
        depth_x = depth[0:4] + depth[1:5]
        lead_y = (lead_x + next_row(lead_x)) + (side_x - next_row(side_x))
        depth_y = depth_x + next_row(depth_x)
        force = (lead_y - depth_y) + from_far(lead_y + depth_y)
        out.append(force[:, 0:8] - near_ref[c, 1:5, 1:9, :] * damp)
    return out


def internal_first_kernel(near, other, out, moduli):
    lame = element_moduli(near[3], other[3])
    shear = element_moduli(near[4], other[4])
    moduli[0] = lame
    moduli[1] = shear
    for c, force in enumerate(internal_force(near, other, lame, shear)):
        out[c] = force


def internal_kernel(near, other, moduli, out):
    for c, force in enumerate(internal_force(near, other, moduli[0], moduli[1])):
        out[c] = force


def column_to_row(column):
    size = column.shape[0]
    eye = iota((size, size), 0) == iota((size, size), 1)
    return jnp.sum(jnp.where(eye, column, 0.0), axis=0, keepdims=True)


def row_to_column(row):
    size = row.shape[1]
    eye = iota((size, size), 0) == iota((size, size), 1)
    return jnp.sum(jnp.where(eye, row, 0.0), axis=1, keepdims=True)


def request_kernel(u, slaves, gaps, chosen, owners, wanted, send, slot_of, at_slaves):
    owner_row = owners[...].astype(F32)
    owner = row_to_column(owner_row)
    same = (owner == owner_row) & (iota((PAIRS, PAIRS), 1) < iota((PAIRS, PAIRS), 0))
    rank = jnp.max(jnp.where(same, 1.0, 0.0), axis=1, keepdims=True)
    slot = rank * GROUPS + owner
    slot_row = column_to_row(slot)
    slot_of[...] = jnp.where(slot == iota((PAIRS, SLOTS), 1).astype(F32), 1.0, 0.0)
    place = jnp.where(slot_row == iota((SLOTS, PAIRS), 0).astype(F32), 1.0, 0.0).astype(BF16)
    values = gather_nodes(u, slaves[...])
    for c in range(3):
        at_slaves[c] = values[c]
    exact = jnp.concatenate(values + [gaps[...]], axis=1)
    moved = select_dot(place, exact)
    patch = jnp.broadcast_to(row_to_column(wanted[...].astype(F32) + 1.0), (PAIRS, PATCH))
    whole = jnp.concatenate([chosen[...].astype(F32), patch], axis=1).astype(BF16)
    moved_whole = jnp.dot(place, whole, preferred_element_type=F32)
    for t in range(CAP):
        part = slice(t * GROUPS, (t + 1) * GROUPS)
        for c in range(4):
            send[pl.ds(t * 4 + c, GROUPS, stride=12), :] = moved[part, c * 128 : (c + 1) * 128]
        for c in range(2):
            send[pl.ds(8 + t * 2 + c, GROUPS, stride=12), :] = moved_whole[
                part, c * 128 : (c + 1) * 128
            ]


def wanted_rows(arrived):
    patch = jnp.concatenate([every(arrived, 9, 12), every(arrived, 11, 12)], axis=0)
    cand = jnp.concatenate([every(arrived, 8, 12), every(arrived, 10, 12)], axis=0)
    at = (iota((SLOTS, PATCH), 1) % PATCHES + 1).astype(F32)
    onehot = jnp.where(patch == at, 1.0, 0.0).astype(BF16)
    return onehot, cand.astype(I32)


def table_kernel(u, faces, table):
    table[...] = patch_table(u, faces[...])


def reply_kernel(arrived, table, faces, send, face_row, face_lane):
    onehot, cand = wanted_rows(arrived)
    tiles = jnp.dot(onehot, table[...], preferred_element_type=F32)
    for c in range(4):
        picked = lane_pick(tiles[:, c * 128 : (c + 1) * 128], cand)
        for t in range(CAP):
            send[pl.ds(t * 4 + c, GROUPS, stride=8), :] = picked[t * GROUPS : (t + 1) * GROUPS]
    index = jnp.concatenate([faces[...] >> 7, faces[...] & 127], axis=1).astype(F32)
    index = jnp.concatenate(
        [index, jnp.zeros((PATCH - PATCHES, 2 * PATCH), F32)], axis=0
    ).astype(BF16)
    index = jnp.dot(onehot, index, preferred_element_type=F32)
    face_row[...] = lane_pick(index[:, 0:128], cand).astype(I32)
    face_lane[...] = lane_pick(index[:, 128:256], cand).astype(I32)


def owner_forces(values, gap_source, frames, stride, offset, frame_stride, frame_offset, scratch):
    for t in range(CAP):
        u = [every(values, t * offset + c, stride) for c in range(3)]
        gap = every(gap_source, t * 4 + 3, 12)
        frame = [every(frames, t * frame_offset[1] + frame_offset[0] + c, frame_stride) for c in range(4)]
        force = pair_force(u, frame[0:3], frame[3], gap)
        for c in range(3):
            store_parts(scratch, c, t * GROUPS, -0.25 * force[c])


def face_contact(face_row, face_lane, scratch):
    def row_lane(start):
        return face_row[pl.ds(start, 32), :], face_lane[pl.ds(start, 32), :]

    faces = scatter_nodes(SLOTS, row_lane, scratch)
    return [x + down_rows(x, 8) + down_rows(x, 9) + down_rows(x, 1) for x in faces]


def slave_contact(arrived, stride, offset, slot_of, at_slaves, gaps, slaves, scratch):
    onehot = slot_of[...].astype(BF16)
    slots = []
    for c in range(4):
        slots.append(
            jnp.concatenate(
                [every(arrived, t * offset[1] + offset[0] + c, stride) for t in range(CAP)], axis=0
            )
        )
    mine = select_dot(onehot, jnp.concatenate(slots, axis=1))
    frame = [mine[:, c * 128 : (c + 1) * 128] for c in range(4)]
    force = pair_force([at_slaves[c] for c in range(3)], frame[0:3], frame[3], gaps[...])
    for c in range(3):
        store_parts(scratch, c, 0, force[c])

    def row_lane(start):
        nodes = slaves[pl.ds(start, 32), :]
        return nodes >> 7, nodes & 127

    return scatter_nodes(PAIRS, row_lane, scratch)


def reaction_kernel(arrived, frames, face_row, face_lane, out, scratch):
    owner_forces(arrived, arrived, frames, 12, 4, 8, (0, 4), scratch)
    for c, force in enumerate(face_contact(face_row, face_lane, scratch)):
        out[c] = force


def advance(c, force, disp, vel, mass, new_disp, new_vel):
    moved = vel[c] + TIME_STEP * force / mass[...]
    new_vel[c] = moved
    place = disp[c] + TIME_STEP * moved
    new_disp[c] = place
    return place


def middle_kernel(
    arrived, slot_of, at_slaves, gaps, slaves, reaction, internal, disp, vel, mass,
    new_disp, new_vel, low, high, scratch,
):
    contact = slave_contact(arrived, 8, (0, 4), slot_of, at_slaves, gaps, slaves, scratch)
    for c in range(3):
        force = internal[c] + (contact[c] + reaction[c])
        place = advance(c, force, disp, vel, mass, new_disp, new_vel)
        low[c] = place[0:NJ]
        high[c] = place[ROWS - NJ : ROWS]


def second_kernel(u, slaves, faces, slot_of, arrived, send, at_slaves):
    values = gather_nodes(u, slaves[...])
    for c in range(3):
        at_slaves[c] = values[c]
    place = slot_of[...].astype(BF16)
    high, mid, low = parts_3(jnp.concatenate(values, axis=1))
    dims = (((0,), (0,)), ((), ()))
    moved = lax.dot_general(place, low, dims, preferred_element_type=F32)
    moved = moved + lax.dot_general(place, mid, dims, preferred_element_type=F32)
    moved = moved + lax.dot_general(place, high, dims, preferred_element_type=F32)
    table = patch_table(u, faces[...])
    onehot, cand = wanted_rows(arrived)
    tiles = jnp.dot(onehot, table, preferred_element_type=F32)
    for t in range(CAP):
        part = slice(t * GROUPS, (t + 1) * GROUPS)
        for c in range(3):
            send[pl.ds(t * 7 + c, GROUPS, stride=14), :] = moved[part, c * 128 : (c + 1) * 128]
    for c in range(4):
        picked = lane_pick(tiles[:, c * 128 : (c + 1) * 128], cand)
        for t in range(CAP):
            send[pl.ds(t * 7 + 3 + c, GROUPS, stride=14), :] = picked[
                t * GROUPS : (t + 1) * GROUPS
            ]


def last_kernel(
    arrived, sent, first, face_row, face_lane, slot_of, at_slaves, gaps, slaves, internal,
    disp, vel, mass, new_disp, new_vel, scratch, slave_scratch,
):
    owner_forces(arrived, first, sent, 14, 7, 14, (3, 7), scratch)
    reaction = face_contact(face_row, face_lane, scratch)
    contact = slave_contact(arrived, 14, (3, 7), slot_of, at_slaves, gaps, slaves, slave_scratch)
    for c in range(3):
        force = internal[c] + (contact[c] + reaction[c])
        advance(c, force, disp, vel, mass, new_disp, new_vel)


def f32(*shape):
    return pltpu.VMEM(shape, F32)


def i32(*shape):
    return pltpu.VMEM(shape, I32)


def plain(*shape):
    return jax.ShapeDtypeStruct(shape, F32)


def call(kernel, outs, *args, scratch=(), raw=0):
    local = pl.BlockSpec(memory_space=pltpu.VMEM)
    whole = pl.BlockSpec()
    inputs = [
        x if i < raw else pltpu.with_memory_space_constraint(x, pltpu.VMEM)
        for i, x in enumerate(args)
    ]
    return pl.pallas_call(
        kernel,
        out_shape=outs,
        in_specs=[whole if i < raw else local for i in range(len(args))],
        out_specs=jax.tree.map(
            lambda x: whole if isinstance(x, jax.ShapeDtypeStruct) else local, outs
        ),
        scratch_shapes=[pltpu.VMEM(s, F32) for s in scratch],
    )(*inputs)


def shift_pair(low, high, axis):
    count = lax.axis_size(axis)
    from_low = lax.ppermute(high, axis, [(i, (i + 1) % count) for i in range(count)])
    from_high = lax.ppermute(low, axis, [((i + 1) % count, i) for i in range(count)])
    return from_low, from_high


def extended(block, low, high):
    parts = block.shape[0]
    x_low, x_high = shift_pair(low, high, "len")
    low, high = call(rim_kernel, (f32(parts, 8, NK), f32(parts, 8, NK)), block, x_low, x_high)
    y_low, y_high = shift_pair(low, high, "wid")
    near = call(
        extend_kernel, f32(parts, NI + 2, 16, NK), block, x_low, x_high, y_low, y_high
    )
    other = lax.ppermute(near, "lay", [(0, 1), (1, 0)])
    return near, other


def exchange(buffer):
    chunk = buffer.reshape(GROUPS, 1, -1)
    out = lax.all_to_all(chunk, ("len", "wid"), split_axis=0, concat_axis=0, tiled=True)
    return out.reshape(buffer.shape)


def program(
    displacement, velocity, lame_first, shear_modulus, nodal_mass, slave_nodes, initial_gap,
    candidate, pair_owner, pair_patch, master_faces,
):
    slaves = slave_nodes.reshape(PAIRS, PATCH)
    gaps = initial_gap.reshape(PAIRS, PATCH)
    chosen = candidate.reshape(PAIRS, PATCH)
    owners = pair_owner.reshape(1, PAIRS)
    wanted = pair_patch.reshape(1, PAIRS)
    faces = master_faces.reshape(PATCHES, PATCH)
    u = displacement.reshape(3, ROWS, NK)
    v = velocity.reshape(3, ROWS, NK)
    mass = nodal_mass.reshape(ROWS, NK)
    five, low, high = call(
        slabs_kernel,
        (f32(5, NI, NJ, NK), f32(5, NJ, NK), f32(5, NJ, NK)),
        displacement, lame_first, shear_modulus, raw=3,
    )
    near, other = extended(five, low, high)
    send, slot_of, at_slaves = call(
        request_kernel,
        (plain(GROUPS * 12, PATCH), f32(PAIRS, SLOTS), f32(3, PAIRS, PATCH)),
        u, slaves, gaps, chosen, owners, wanted, raw=6,
    )
    first = exchange(send)
    table = call(table_kernel, pltpu.VMEM((128, 512), BF16), u, faces)
    reply, face_row, face_lane = call(
        reply_kernel,
        (plain(GROUPS * 8, PATCH), i32(SLOTS, PATCH), i32(SLOTS, PATCH)),
        first, table, faces,
    )
    arrived = exchange(reply)
    reaction = call(
        reaction_kernel, f32(3, ROWS, NK), first, reply, face_row, face_lane,
        scratch=[(6, SLOTS, PATCH)],
    )
    internal, moduli = call(
        internal_first_kernel, (f32(3, NI, NJ, NK), f32(2, 5, 16, NK)), near, other
    )
    u, v, low, high = call(
        middle_kernel,
        (f32(3, ROWS, NK), f32(3, ROWS, NK), f32(3, NJ, NK), f32(3, NJ, NK)),
        arrived, slot_of, at_slaves, gaps, slaves, reaction, internal.reshape(3, ROWS, NK),
        u, v, mass,
        scratch=[(6, PAIRS, PATCH)],
    )
    near, other = extended(u.reshape(3, NI, NJ, NK), low, high)
    sent, at_slaves = call(
        second_kernel,
        (plain(GROUPS * 14, PATCH), f32(3, PAIRS, PATCH)),
        u, slaves, faces, slot_of, first,
    )
    arrived = exchange(sent)
    internal = call(internal_kernel, f32(3, NI, NJ, NK), near, other, moduli)
    u, v = call(
        last_kernel,
        (plain(3, ROWS, NK), plain(3, ROWS, NK)),
        arrived, sent, first, face_row, face_lane, slot_of, at_slaves, gaps, slaves,
        internal.reshape(3, ROWS, NK), u, v, mass,
        scratch=[(6, SLOTS, PATCH), (6, PAIRS, PATCH)],
    )
    return u.reshape(displacement.shape), v.reshape(velocity.shape)


def solution(mesh):
    nodal = P("len", "wid", "lay")
    vector = P(None, "len", "wid", "lay")
    in_specs = (
        vector, vector, nodal, nodal, nodal,
        P("len", "wid", "lay", None, None),
        P("len", "wid", "lay", None, None),
        P("len", "wid", "lay", None, None),
        P("len", "wid", "lay", None, None),
        P("len", "wid", "lay", None),
        P("len", "wid", "lay", None, None),
    )
    return jax.shard_map(
        program, mesh=mesh, in_specs=in_specs, out_specs=(vector, vector), check_vma=False
    )
```

```python
import jax
import jax.numpy as jnp
from jax import lax
from jax.experimental import pallas as pl
from jax.experimental.pallas import tpu as pltpu
from jax.sharding import PartitionSpec as P


PENALTY = 4.0
HOURGLASS = 0.3
TIME_STEP = 0.25

NI, NJ, NK = 4, 8, 128
ROWS = NI * NJ
PAIRS = 64
PATCH = 128
PATCHES = 32
GROUPS = 64
CAP = 2
SLOTS = GROUPS * CAP
F32 = jnp.float32
BF16 = jnp.bfloat16
I32 = jnp.int32


def iota(shape, axis):
    return lax.broadcasted_iota(I32, shape, axis)


def lane_pick(values, index):
    return jnp.take_along_axis(values, index, axis=1, mode="promise_in_bounds")


def parts_3(x):
    high = x.astype(BF16)
    rest = x - high.astype(F32)
    mid = rest.astype(BF16)
    low = (rest - mid.astype(F32)).astype(BF16)
    return high, mid, low


def select_dot(onehot, x):
    high, mid, low = parts_3(x)
    out = jnp.dot(onehot, low, preferred_element_type=F32)
    out = out + jnp.dot(onehot, mid, preferred_element_type=F32)
    return out + jnp.dot(onehot, high, preferred_element_type=F32)


def gather_nodes(u_ref, slaves, out_ref):
    def body(i, carry):
        start = pl.multiple_of(i * 8, 8)
        nodes = slaves[pl.ds(start, 8), :]
        row = nodes >> 7
        lane = nodes & 127
        out = [jnp.zeros((8, PATCH), F32) for _ in range(3)]
        for r in range(ROWS):
            here = row == r
            for c in range(3):
                source = jnp.broadcast_to(u_ref[c, r : r + 1, :], (8, PATCH))
                out[c] = jnp.where(here, lane_pick(source, lane), out[c])
        for c in range(3):
            out_ref[c, pl.ds(start, 8), :] = out[c]
        return carry

    lax.fori_loop(0, PAIRS // 8, body, 0)


def up(x, amount):
    return pltpu.roll(x, x.shape[0] - amount, 0)


def patch_table(u_ref, faces, normals):
    frames = []
    one = [u_ref[c] for c in range(3)]
    two = [up(x, 8) for x in one]
    three = [up(x, 9) for x in one]
    four = [up(x, 1) for x in one]
    centroid = [(one[c] + two[c] + three[c] + four[c]) * 0.25 for c in range(3)]
    da = [three[0] - one[0] + 1.0, three[1] - one[1] + 1.0, three[2] - one[2]]
    db = [four[0] - two[0] - 1.0, four[1] - two[1] + 1.0, four[2] - two[2]]
    normal = [
        da[1] * db[2] - da[2] * db[1],
        da[2] * db[0] - da[0] * db[2],
        da[0] * db[1] - da[1] * db[0],
    ]
    length = jnp.sqrt(normal[0] * normal[0] + normal[1] * normal[1] + normal[2] * normal[2])
    normal = [x / length for x in normal]
    offset = centroid[0] * normal[0] + centroid[1] * normal[1] + centroid[2] * normal[2]
    frames = normal + [offset]
    for c in range(3):
        normals[c] = normal[c]
    out = [[] for _ in range(4)]
    for start in range(0, PATCHES, 8):
        row = faces[start : start + 8] >> 7
        lane = faces[start : start + 8] & 127
        best = [jnp.zeros((8, PATCH), F32) for _ in range(4)]
        for r in range((NI - 1) * NJ):
            if r % NJ == NJ - 1:
                continue
            here = row == r
            for c in range(4):
                source = jnp.broadcast_to(frames[c][r : r + 1, :], (8, PATCH))
                best[c] = jnp.where(here, lane_pick(source, lane), best[c])
        for c in range(4):
            out[c].append(best[c])
    out = [jnp.concatenate(x, axis=0) for x in out]
    table = jnp.concatenate(out, axis=1)
    high, mid, low = parts_3(table)
    return jnp.concatenate([high, mid, low, jnp.zeros_like(high)], axis=0)


def packed_row(x, q):
    return jnp.broadcast_to(x[q : q + 1, :], (16, PATCH)).astype(BF16)


def scatter_nodes(count, row_lane, forces_ref):
    pieces_count = forces_ref.shape[0]
    parts_count = pieces_count // 2
    half = ROWS // 2
    row_at = iota((half, PATCH), 0).astype(F32).astype(BF16)
    lane_at = iota((2 * PATCH, PATCH), 0).astype(F32).astype(BF16)
    none = jnp.zeros((half, PATCH), BF16)

    def body(i, acc):
        start = pl.multiple_of(i * 32, 32)
        rows, lanes = row_lane(start)
        lanes = (lanes + (rows >> 4) * PATCH).astype(F32)
        rows = (rows & (half - 1)).astype(F32)
        parts = [forces_ref[c, pl.ds(start, 32), :] for c in range(pieces_count)]
        left = []
        right = []
        for q in range(32):
            here = packed_row(rows, q) == row_at
            pieces = [jnp.where(here, packed_row(part, q), none) for part in parts]
            left.append(jnp.concatenate(pieces, axis=0))
            chosen = jnp.concatenate([packed_row(lanes, q)] * 16, axis=0) == lane_at
            right.append(jnp.where(chosen, jnp.ones_like(lane_at), jnp.zeros_like(lane_at)))
        left = jnp.concatenate(left, axis=1)
        right = jnp.concatenate(right, axis=1)
        return acc + lax.dot_general(
            left, right, (((1,), (1,)), ((), ())), preferred_element_type=F32
        )

    acc = lax.fori_loop(0, count // 32, body, jnp.zeros((pieces_count * half, 2 * PATCH), F32))
    acc = acc[0 : parts_count * half] + acc[parts_count * half : pieces_count * half]
    out = []
    for c in range(parts_count):
        part = acc[c * half : (c + 1) * half]
        out.append(jnp.concatenate([part[:, 0:PATCH], part[:, PATCH:]], axis=0))
    return out


def store_parts(forces_ref, c, start, force):
    high = force.astype(BF16).astype(F32)
    forces_ref[c, start : start + force.shape[0], :] = high
    low = c + forces_ref.shape[0] // 2
    forces_ref[low, start : start + force.shape[0], :] = force - high


def down_rows(x, amount):
    moved = pltpu.roll(x, amount, 0)
    return jnp.where(iota(x.shape, 0) >= amount, moved, 0.0)


def pair_push(u, normal, offset, gap):
    now = gap + (u[0] * normal[0] + u[1] * normal[1] + u[2] * normal[2]) - offset
    return -PENALTY * jnp.minimum(now, 0.0)


def every(ref, start, stride):
    return ref[pl.ds(start, GROUPS, stride=stride), :]


def is_even(axis):
    return lax.axis_index(axis) % 2 == 0


def store_faces(axis, first, second, at, low, high):
    even = is_even(axis)
    first[at] = jnp.where(even, high, low)
    second[at] = jnp.where(even, low, high)


def low_high(axis, first, second):
    even = is_even(axis)
    return jnp.where(even, second, first), jnp.where(even, first, second)


def slabs_kernel(
    disp, lame, shear, vel, mass, faces, five, first, second, vel_out, mass_out, faces_out
):
    vel_out[...] = vel[...]
    mass_out[...] = mass[...]
    faces_out[...] = faces[...]
    for c in range(5):
        block = disp[c] if c < 3 else (lame[...] if c == 3 else shear[...])
        five[c] = block
        store_faces("len", first, second, c, block[0], block[NI - 1])


def widen_kernel(block, x_first, x_second, out):
    for c in range(block.shape[0]):
        out[c, 0], out[c, NI + 1] = low_high("len", x_first[c], x_second[c])
        for i in range(NI):
            out[c, i + 1] = block[c, i]


def face_rows(planes, j):
    rows = [x[j : j + 1, :] for x in planes]
    return jnp.concatenate(rows + [jnp.zeros((8 - len(rows), NK), F32)], axis=0)


def rim_kernel(near, other, first, second):
    for half, source in enumerate((near, other)):
        for c in range(source.shape[0]):
            planes = [source[c, i] for i in range(NI + 2)]
            low, high = face_rows(planes, 0), face_rows(planes, NJ - 1)
            store_faces("wid", first, second, half * source.shape[0] + c, low, high)


def ring_kernel(block, x_first, x_second, first, second):
    for c in range(block.shape[0]):
        x_low, x_high = low_high("len", x_first[c], x_second[c])
        planes = [x_low] + [block[c, i] for i in range(NI)] + [x_high]
        store_faces("wid", first, second, c, face_rows(planes, 0), face_rows(planes, NJ - 1))


def put_planes(out, c, planes, first, second):
    low, high = low_high("wid", first, second)
    for i, plane in enumerate(planes):
        out[c, i, 1:9, :] = plane
        out[c, i, 0:1, :] = low[i : i + 1, :]
        out[c, i, 9:10, :] = high[i : i + 1, :]
        out[c, i, 10:16, :] = jnp.zeros((6, NK), F32)


def extend(source, first, second, half, out):
    for c in range(source.shape[0]):
        at = half * source.shape[0] + c
        put_planes(out, c, [source[c, i] for i in range(NI + 2)], first[at], second[at])


def extend_kernel(block, x_first, x_second, y_first, y_second, out):
    for c in range(block.shape[0]):
        x_low, x_high = low_high("len", x_first[c], x_second[c])
        planes = [x_low] + [block[c, i] for i in range(NI)] + [x_high]
        put_planes(out, c, planes, y_first[c], y_second[c])


def far_plane(near, other):
    lay = lax.axis_index("lay")
    lane = iota(near.shape, 2)
    edge = jnp.where(lay == 0, 0, NK - 1)
    shift = jnp.where(lay == 0, NK - 1, 1)
    return pltpu.roll(jnp.where(lane == edge, other, near), shift, 2)


def from_far(x):
    lay = lax.axis_index("lay")
    lane = iota(x.shape, 2)
    edge = jnp.where(lay == 0, 0, NK - 1)
    shift = jnp.where(lay == 0, 1, NK - 1)
    return jnp.where(lane == edge, 0.0, pltpu.roll(x, shift, 2))


def next_row(x):
    return pltpu.roll(x, x.shape[1] - 1, 1)


def element_moduli(near, other):
    total = near + far_plane(near, other)
    total = total + next_row(total)
    total = (total[0:5] + total[1:6]) * 0.125
    plane = iota(total.shape, 0)
    row = iota(total.shape, 1)
    at_len = lax.axis_index("len")
    at_wid = lax.axis_index("wid")
    outside = (plane == 0) & (at_len == 0)
    outside |= (plane == NI) & (at_len == lax.axis_size("len") - 1)
    outside |= (row == 0) & (at_wid == 0)
    outside |= (row == NJ) & (at_wid == lax.axis_size("wid") - 1)
    return jnp.where(outside, 0.0, total)


def internal_force(near_ref, other_ref, lame, shear):
    sigma = jnp.where(lax.axis_index("lay") == 0, 1.0, -1.0)
    grad = []
    means = []
    for c in range(3):
        near = near_ref[c]
        far = far_plane(near, other_ref[c])
        both = far + near
        diff = far - near
        both_next = next_row(both)
        sums = both + both_next
        cross = both_next - both
        tall = diff + next_row(diff)
        means.append((sums[0:5] + sums[1:6]) * 0.125)
        grad.append(
            [
                (sums[1:6] - sums[0:5]) * 0.25,
                (cross[0:5] + cross[1:6]) * 0.25,
                (tall[0:5] + tall[1:6]) * (0.25 * sigma),
            ]
        )
    pressure = lame * (grad[0][0] + grad[1][1] + grad[2][2])
    damping = HOURGLASS * shear
    damp_x = damping[0:4] + damping[1:5]
    damp_y = damp_x + next_row(damp_x)
    damp = (damp_y + from_far(damp_y))[:, 0:8]
    out = []
    for c in range(3):
        flux = []
        for j in range(3):
            stress = shear * (grad[c][j] + grad[j][c])
            if c == j:
                stress = stress + pressure
            flux.append(0.5 * damping * grad[c][j] - 0.25 * stress)
        lead = damping * means[c]
        depth = flux[2] * sigma
        lead_x = (lead[0:4] + lead[1:5]) + (flux[0][0:4] - flux[0][1:5])
        side_x = flux[1][0:4] + flux[1][1:5]
        depth_x = depth[0:4] + depth[1:5]
        lead_y = (lead_x + next_row(lead_x)) + (side_x - next_row(side_x))
        depth_y = depth_x + next_row(depth_x)
        force = (lead_y - depth_y) + from_far(lead_y + depth_y)
        out.append(force[:, 0:8] - near_ref[c, 1:5, 1:9, :] * damp)
    return out


def internal_first_kernel(near, other, y_low, y_high, out, moduli, here, there):
    extend(near, y_low, y_high, 0, here)
    extend(other, y_low, y_high, 1, there)
    lame = element_moduli(here[3], there[3])
    shear = element_moduli(here[4], there[4])
    moduli[0] = lame
    moduli[1] = shear
    for c, force in enumerate(internal_force(here, there, lame, shear)):
        out[c] = force


def column_to_row(column):
    size = column.shape[0]
    eye = iota((size, size), 0) == iota((size, size), 1)
    return jnp.sum(jnp.where(eye, column, 0.0), axis=0, keepdims=True)


def row_to_column(row):
    size = row.shape[1]
    eye = iota((size, size), 0) == iota((size, size), 1)
    return jnp.sum(jnp.where(eye, row, 0.0), axis=1, keepdims=True)


def request_kernel(
    u, slaves, gaps, chosen, owners, wanted, send, slot_of, at_slaves, slaves_out, gaps_out
):
    slaves_out[...] = slaves[...]
    gaps_out[...] = gaps[...]
    owner_row = owners[...].astype(F32)
    owner = row_to_column(owner_row)
    same = (owner == owner_row) & (iota((PAIRS, PAIRS), 1) < iota((PAIRS, PAIRS), 0))
    rank = jnp.max(jnp.where(same, 1.0, 0.0), axis=1, keepdims=True)
    slot = rank * GROUPS + owner
    slot_row = column_to_row(slot)
    slot_of[...] = jnp.where(slot == iota((PAIRS, SLOTS), 1).astype(F32), 1.0, 0.0)
    place = jnp.where(slot_row == iota((SLOTS, PAIRS), 0).astype(F32), 1.0, 0.0).astype(BF16)
    gather_nodes(u, slaves, at_slaves)
    values = [at_slaves[c] for c in range(3)]
    exact = jnp.concatenate(values + [gaps[...]], axis=1)
    moved = select_dot(place, exact)
    patch = jnp.broadcast_to(row_to_column(wanted[...].astype(F32) + 1.0), (PAIRS, PATCH))
    whole = jnp.concatenate([chosen[...].astype(F32), patch], axis=1).astype(BF16)
    moved_whole = jnp.dot(place, whole, preferred_element_type=F32)
    for t in range(CAP):
        part = slice(t * GROUPS, (t + 1) * GROUPS)
        for c in range(4):
            send[pl.ds(t * 4 + c, GROUPS, stride=12), :] = moved[part, c * 128 : (c + 1) * 128]
        for c in range(2):
            send[pl.ds(8 + t * 2 + c, GROUPS, stride=12), :] = moved_whole[
                part, c * 128 : (c + 1) * 128
            ]


def wanted_rows(arrived):
    patch = jnp.concatenate([every(arrived, 9, 12), every(arrived, 11, 12)], axis=0)
    cand = jnp.concatenate([every(arrived, 8, 12), every(arrived, 10, 12)], axis=0)
    at = (iota((SLOTS, PATCH), 1) % PATCHES + 1).astype(F32)
    onehot = jnp.where(patch == at, 1.0, 0.0).astype(BF16)
    return onehot, cand.astype(I32)


def table_kernel(u, faces, table, normals):
    table[...] = patch_table(u, faces[...], normals)


def reply_kernel(arrived, table, faces, send, face_row, face_lane):
    onehot, cand = wanted_rows(arrived)
    tiles = jnp.dot(onehot, table[...], preferred_element_type=F32)
    for c in range(4):
        picked = lane_pick(tiles[:, c * 128 : (c + 1) * 128], cand)
        for t in range(CAP):
            send[pl.ds(t * 4 + c, GROUPS, stride=8), :] = picked[t * GROUPS : (t + 1) * GROUPS]
    index = jnp.concatenate([faces[...] >> 7, faces[...] & 127], axis=1).astype(F32)
    index = jnp.concatenate(
        [index, jnp.zeros((PATCH - PATCHES, 2 * PATCH), F32)], axis=0
    ).astype(BF16)
    index = jnp.dot(onehot, index, preferred_element_type=F32)
    face_row[...] = lane_pick(index[:, 0:128], cand).astype(I32)
    face_lane[...] = lane_pick(index[:, 128:256], cand).astype(I32)


def owner_forces(values, gap_source, frames, stride, offset, frame_stride, frame_offset, scratch):
    for t in range(CAP):
        u = [every(values, t * offset + c, stride) for c in range(3)]
        gap = every(gap_source, t * 4 + 3, 12)
        frame = [every(frames, t * frame_offset[1] + frame_offset[0] + c, frame_stride) for c in range(4)]
        push = pair_push(u, frame[0:3], frame[3], gap)
        store_parts(scratch, 0, t * GROUPS, -0.25 * push)


def face_contact(face_row, face_lane, normals, scratch):
    def row_lane(start):
        return face_row[pl.ds(start, 32), :], face_lane[pl.ds(start, 32), :]

    (push,) = scatter_nodes(SLOTS, row_lane, scratch)
    out = []
    for c in range(3):
        x = jnp.where(push == 0.0, 0.0, push * normals[c])
        out.append(x + down_rows(x, 8) + down_rows(x, 9) + down_rows(x, 1))
    return out


def slave_contact(arrived, stride, offset, slot_of, at_slaves, gaps, slaves, scratch):
    onehot = slot_of[...].astype(BF16)
    slots = []
    for c in range(4):
        slots.append(
            jnp.concatenate(
                [every(arrived, t * offset[1] + offset[0] + c, stride) for t in range(CAP)], axis=0
            )
        )
    mine = select_dot(onehot, jnp.concatenate(slots, axis=1))
    frame = [mine[:, c * 128 : (c + 1) * 128] for c in range(4)]
    push = pair_push([at_slaves[c] for c in range(3)], frame[0:3], frame[3], gaps[...])
    for c in range(3):
        store_parts(scratch, c, 0, push * frame[c])

    def row_lane(start):
        nodes = slaves[pl.ds(start, 32), :]
        return nodes >> 7, nodes & 127

    return scatter_nodes(PAIRS, row_lane, scratch)


def reaction_kernel(arrived, frames, face_row, face_lane, normals, out, scratch):
    owner_forces(arrived, arrived, frames, 12, 4, 8, (0, 4), scratch)
    for c, force in enumerate(face_contact(face_row, face_lane, normals, scratch)):
        out[c] = force


def advance(c, force, disp, vel, mass, new_disp, new_vel):
    moved = vel[c] + TIME_STEP * force / mass[...]
    new_vel[c] = moved
    place = disp[c] + TIME_STEP * moved
    new_disp[c] = place
    return place


def middle_kernel(
    arrived, slot_of, at_slaves, gaps, slaves, reaction, internal, disp, vel, mass,
    new_disp, new_vel, first, second, scratch,
):
    contact = slave_contact(arrived, 8, (0, 4), slot_of, at_slaves, gaps, slaves, scratch)
    for c in range(3):
        force = internal[c] + (contact[c] + reaction[c])
        place = advance(c, force, disp, vel, mass, new_disp, new_vel)
        store_faces("len", first, second, c, place[0:NJ], place[ROWS - NJ : ROWS])


def second_kernel(u, slaves, faces, slot_of, arrived, send, at_slaves, normals):
    gather_nodes(u, slaves, at_slaves)
    values = [at_slaves[c] for c in range(3)]
    place = slot_of[...].astype(BF16)
    high, mid, low = parts_3(jnp.concatenate(values, axis=1))
    dims = (((0,), (0,)), ((), ()))
    moved = lax.dot_general(place, low, dims, preferred_element_type=F32)
    moved = moved + lax.dot_general(place, mid, dims, preferred_element_type=F32)
    moved = moved + lax.dot_general(place, high, dims, preferred_element_type=F32)
    table = patch_table(u, faces[...], normals)
    onehot, cand = wanted_rows(arrived)
    tiles = jnp.dot(onehot, table, preferred_element_type=F32)
    for t in range(CAP):
        part = slice(t * GROUPS, (t + 1) * GROUPS)
        for c in range(3):
            send[pl.ds(t * 7 + c, GROUPS, stride=14), :] = moved[part, c * 128 : (c + 1) * 128]
    for c in range(4):
        picked = lane_pick(tiles[:, c * 128 : (c + 1) * 128], cand)
        for t in range(CAP):
            send[pl.ds(t * 7 + 3 + c, GROUPS, stride=14), :] = picked[
                t * GROUPS : (t + 1) * GROUPS
            ]


def contact_kernel(
    arrived, sent, first, face_row, face_lane, normals, slot_of, at_slaves, gaps, slaves, out,
    scratch, slave_scratch,
):
    owner_forces(arrived, first, sent, 14, 7, 14, (3, 7), scratch)
    reaction = face_contact(face_row, face_lane, normals, scratch)
    contact = slave_contact(arrived, 14, (3, 7), slot_of, at_slaves, gaps, slaves, slave_scratch)
    for c in range(3):
        out[c] = contact[c] + reaction[c]


def finish_kernel(near, other, moduli, contact, disp, vel, mass, new_disp, new_vel):
    for c, internal in enumerate(internal_force(near, other, moduli[0], moduli[1])):
        moved = vel[c] + TIME_STEP * (internal + contact[c]) / mass[...]
        new_vel[c] = moved
        new_disp[c] = disp[c] + TIME_STEP * moved


def f32(*shape):
    return pltpu.VMEM(shape, F32)


def i32(*shape):
    return pltpu.VMEM(shape, I32)


def plain(*shape):
    return jax.ShapeDtypeStruct(shape, F32)


def call(kernel, outs, *args, scratch=(), raw=0):
    local = pl.BlockSpec(memory_space=pltpu.VMEM)
    whole = pl.BlockSpec()
    inputs = [
        x if i < raw else pltpu.with_memory_space_constraint(x, pltpu.VMEM)
        for i, x in enumerate(args)
    ]
    return pl.pallas_call(
        kernel,
        out_shape=outs,
        in_specs=[whole if i < raw else local for i in range(len(args))],
        out_specs=jax.tree.map(
            lambda x: whole if isinstance(x, jax.ShapeDtypeStruct) else local, outs
        ),
        scratch_shapes=[pltpu.VMEM(s, F32) for s in scratch],
    )(*inputs)


def swap_pair(first, second, axis):
    count = lax.axis_size(axis)
    mate = [(i, i ^ 1) for i in range(count)]
    other = [(i, (i - 1 if i % 2 == 0 else i + 1) % count) for i in range(count)]
    return lax.ppermute(first, axis, mate), lax.ppermute(second, axis, other)


def surroundings(block, low, high):
    parts = block.shape[0]
    x_low, x_high = swap_pair(low, high, "len")
    near = call(widen_kernel, f32(parts, NI + 2, NJ, NK), block, x_low, x_high)
    other = lax.ppermute(near, "lay", [(0, 1), (1, 0)])
    low, high = call(rim_kernel, (f32(2 * parts, 8, NK), f32(2 * parts, 8, NK)), near, other)
    y_low, y_high = swap_pair(low, high, "wid")
    return near, other, y_low, y_high


def extended(block, low, high):
    x_low, x_high = swap_pair(low, high, "len")
    low, high = call(ring_kernel, (f32(3, 8, NK), f32(3, 8, NK)), block, x_low, x_high)
    y_low, y_high = swap_pair(low, high, "wid")
    near = call(extend_kernel, f32(3, NI + 2, 16, NK), block, x_low, x_high, y_low, y_high)
    other = lax.ppermute(near, "lay", [(0, 1), (1, 0)])
    return near, other


def exchange(buffer):
    chunk = buffer.reshape(GROUPS, 1, -1)
    out = lax.all_to_all(chunk, ("len", "wid"), split_axis=0, concat_axis=0, tiled=True)
    return out.reshape(buffer.shape)


def program(
    displacement, velocity, lame_first, shear_modulus, nodal_mass, slave_nodes, initial_gap,
    candidate, pair_owner, pair_patch, master_faces,
):
    slaves = slave_nodes.reshape(PAIRS, PATCH)
    gaps = initial_gap.reshape(PAIRS, PATCH)
    chosen = candidate.reshape(PAIRS, PATCH)
    owners = pair_owner.reshape(1, PAIRS)
    wanted = pair_patch.reshape(1, PAIRS)
    faces = master_faces.reshape(PATCHES, PATCH)
    u = displacement.reshape(3, ROWS, NK)
    v = velocity.reshape(3, ROWS, NK)
    mass = nodal_mass.reshape(ROWS, NK)
    five, low, high, v, mass, faces = call(
        slabs_kernel,
        (
            f32(5, NI, NJ, NK), f32(5, NJ, NK), f32(5, NJ, NK), f32(3, ROWS, NK), f32(ROWS, NK),
            i32(PATCHES, PATCH),
        ),
        displacement, lame_first, shear_modulus, v, mass, faces, raw=6,
    )
    around = surroundings(five, low, high)
    send, slot_of, at_slaves, slaves, gaps = call(
        request_kernel,
        (
            plain(GROUPS * 12, PATCH), f32(PAIRS, SLOTS), f32(3, PAIRS, PATCH),
            i32(PAIRS, PATCH), f32(PAIRS, PATCH),
        ),
        u, slaves, gaps, chosen, owners, wanted, raw=6,
    )
    first = exchange(send)
    table, normals = call(
        table_kernel, (pltpu.VMEM((128, 512), BF16), f32(3, ROWS, NK)), u, faces
    )
    reply, face_row, face_lane = call(
        reply_kernel,
        (plain(GROUPS * 8, PATCH), i32(SLOTS, PATCH), i32(SLOTS, PATCH)),
        first, table, faces,
    )
    arrived = exchange(reply)
    reaction = call(
        reaction_kernel, f32(3, ROWS, NK), first, reply, face_row, face_lane, normals,
        scratch=[(2, SLOTS, PATCH)],
    )
    internal, moduli = call(
        internal_first_kernel, (f32(3, NI, NJ, NK), f32(2, 5, 16, NK)), *around,
        scratch=[(5, NI + 2, 16, NK)] * 2,
    )
    u, v, low, high = call(
        middle_kernel,
        (f32(3, ROWS, NK), f32(3, ROWS, NK), f32(3, NJ, NK), f32(3, NJ, NK)),
        arrived, slot_of, at_slaves, gaps, slaves, reaction, internal.reshape(3, ROWS, NK),
        u, v, mass,
        scratch=[(6, PAIRS, PATCH)],
    )
    near, other = extended(u.reshape(3, NI, NJ, NK), low, high)
    sent, at_slaves, next_normals = call(
        second_kernel,
        (plain(GROUPS * 14, PATCH), f32(3, PAIRS, PATCH), f32(3, ROWS, NK)),
        u, slaves, faces, slot_of, first,
    )
    arrived = exchange(sent)
    contact = call(
        contact_kernel, f32(3, ROWS, NK),
        arrived, sent, first, face_row, face_lane, next_normals, slot_of, at_slaves, gaps, slaves,
        scratch=[(2, SLOTS, PATCH), (6, PAIRS, PATCH)],
    )
    block = (3, NI, NJ, NK)
    u, v = call(
        finish_kernel, (plain(*block), plain(*block)),
        near, other, moduli, contact.reshape(block), u.reshape(block), v.reshape(block),
        mass.reshape(NI, NJ, NK),
    )
    return u.reshape(displacement.shape), v.reshape(velocity.shape)


def solution(mesh):
    nodal = P("len", "wid", "lay")
    vector = P(None, "len", "wid", "lay")
    in_specs = (
        vector, vector, nodal, nodal, nodal,
        P("len", "wid", "lay", None, None),
        P("len", "wid", "lay", None, None),
        P("len", "wid", "lay", None, None),
        P("len", "wid", "lay", None, None),
        P("len", "wid", "lay", None),
        P("len", "wid", "lay", None, None),
    )
    return jax.shard_map(
        program, mesh=mesh, in_specs=in_specs, out_specs=(vector, vector), check_vma=False
    )
```

```python
import jax
import jax.numpy as jnp
from jax import lax
from jax.experimental import pallas as pl
from jax.experimental.pallas import tpu as pltpu
from jax.sharding import PartitionSpec as P


PENALTY = 4.0
HOURGLASS = 0.3
TIME_STEP = 0.25

NI, NJ, NK = 4, 8, 128
ROWS = NI * NJ
PAIRS = 64
PATCH = 128
PATCHES = 32
GROUPS = 64
CAP = 2
SLOTS = GROUPS * CAP
F32 = jnp.float32
BF16 = jnp.bfloat16
I32 = jnp.int32


def iota(shape, axis):
    return lax.broadcasted_iota(I32, shape, axis)


def lane_pick(values, index):
    return jnp.take_along_axis(values, index, axis=1, mode="promise_in_bounds")


def parts_3(x):
    high = x.astype(BF16)
    rest = x - high.astype(F32)
    mid = rest.astype(BF16)
    low = (rest - mid.astype(F32)).astype(BF16)
    return high, mid, low


def select_dot(onehot, x):
    high, mid, low = parts_3(x)
    out = jnp.dot(onehot, low, preferred_element_type=F32)
    out = out + jnp.dot(onehot, mid, preferred_element_type=F32)
    return out + jnp.dot(onehot, high, preferred_element_type=F32)


def gather_nodes(u_ref, slaves, out_ref):
    def body(i, carry):
        start = pl.multiple_of(i * 8, 8)
        nodes = slaves[pl.ds(start, 8), :]
        row = nodes >> 7
        lane = nodes & 127
        out = [jnp.zeros((8, PATCH), F32) for _ in range(3)]
        for r in range(ROWS):
            here = row == r
            for c in range(3):
                source = jnp.broadcast_to(u_ref[c, r : r + 1, :], (8, PATCH))
                out[c] = jnp.where(here, lane_pick(source, lane), out[c])
        for c in range(3):
            out_ref[c, pl.ds(start, 8), :] = out[c]
        return carry

    lax.fori_loop(0, PAIRS // 8, body, 0)


def up(x, amount):
    return pltpu.roll(x, x.shape[0] - amount, 0)


def patch_table(u_ref, faces, normals):
    frames = []
    one = [u_ref[c] for c in range(3)]
    two = [up(x, 8) for x in one]
    three = [up(x, 9) for x in one]
    four = [up(x, 1) for x in one]
    centroid = [(one[c] + two[c] + three[c] + four[c]) * 0.25 for c in range(3)]
    da = [three[0] - one[0] + 1.0, three[1] - one[1] + 1.0, three[2] - one[2]]
    db = [four[0] - two[0] - 1.0, four[1] - two[1] + 1.0, four[2] - two[2]]
    normal = [
        da[1] * db[2] - da[2] * db[1],
        da[2] * db[0] - da[0] * db[2],
        da[0] * db[1] - da[1] * db[0],
    ]
    length = jnp.sqrt(normal[0] * normal[0] + normal[1] * normal[1] + normal[2] * normal[2])
    normal = [x / length for x in normal]
    offset = centroid[0] * normal[0] + centroid[1] * normal[1] + centroid[2] * normal[2]
    frames = normal + [offset]
    for c in range(3):
        normals[c] = normal[c]
    out = [[] for _ in range(4)]
    for start in range(0, PATCHES, 8):
        row = faces[start : start + 8] >> 7
        lane = faces[start : start + 8] & 127
        best = [jnp.zeros((8, PATCH), F32) for _ in range(4)]
        for r in range((NI - 1) * NJ):
            if r % NJ == NJ - 1:
                continue
            here = row == r
            for c in range(4):
                source = jnp.broadcast_to(frames[c][r : r + 1, :], (8, PATCH))
                best[c] = jnp.where(here, lane_pick(source, lane), best[c])
        for c in range(4):
            out[c].append(best[c])
    out = [jnp.concatenate(x, axis=0) for x in out]
    table = jnp.concatenate(out, axis=1)
    high, mid, low = parts_3(table)
    return jnp.concatenate([high, mid, low, jnp.zeros_like(high)], axis=0)


def packed_row(x, q):
    return jnp.broadcast_to(x[q : q + 1, :], (16, PATCH)).astype(BF16)


def scatter_nodes(count, row_lane, forces_ref):
    pieces_count = forces_ref.shape[0]
    parts_count = pieces_count // 2
    size = 64
    row_at = iota((ROWS, PATCH), 0).astype(F32).astype(BF16)
    lane_at = iota((PATCH, PATCH), 0).astype(F32).astype(BF16)
    none = jnp.zeros((ROWS, PATCH), BF16)

    def body(i, acc):
        start = pl.multiple_of(i * size, size)
        rows, lanes = row_lane(start, size)
        rows = rows.astype(F32)
        lanes = lanes.astype(F32)
        parts = [forces_ref[c, pl.ds(start, size), :] for c in range(pieces_count)]
        left = []
        right = []
        for q in range(size):
            here = jnp.concatenate([packed_row(rows, q)] * 2, axis=0) == row_at
            pieces = [
                jnp.where(here, jnp.concatenate([packed_row(part, q)] * 2, axis=0), none)
                for part in parts
            ]
            left.append(jnp.concatenate(pieces, axis=0))
            chosen = jnp.concatenate([packed_row(lanes, q)] * 8, axis=0) == lane_at
            right.append(jnp.where(chosen, jnp.ones_like(lane_at), jnp.zeros_like(lane_at)))
        left = jnp.concatenate(left, axis=1)
        right = jnp.concatenate(right, axis=1)
        return acc + lax.dot_general(
            left, right, (((1,), (1,)), ((), ())), preferred_element_type=F32
        )

    acc = lax.fori_loop(0, count // size, body, jnp.zeros((pieces_count * ROWS, PATCH), F32))
    acc = acc[0 : parts_count * ROWS] + acc[parts_count * ROWS : pieces_count * ROWS]
    return [acc[c * ROWS : (c + 1) * ROWS] for c in range(parts_count)]


def store_parts(forces_ref, c, start, force):
    high = force.astype(BF16).astype(F32)
    forces_ref[c, start : start + force.shape[0], :] = high
    low = c + forces_ref.shape[0] // 2
    forces_ref[low, start : start + force.shape[0], :] = force - high


def down_rows(x, amount):
    moved = pltpu.roll(x, amount, 0)
    return jnp.where(iota(x.shape, 0) >= amount, moved, 0.0)


def pair_push(u, normal, offset, gap):
    now = gap + (u[0] * normal[0] + u[1] * normal[1] + u[2] * normal[2]) - offset
    return -PENALTY * jnp.minimum(now, 0.0)


def every(ref, start, stride):
    return ref[pl.ds(start, GROUPS, stride=stride), :]


def is_even(axis):
    return lax.axis_index(axis) % 2 == 0


def store_faces(axis, first, second, at, low, high):
    even = is_even(axis)
    first[at] = jnp.where(even, high, low)
    second[at] = jnp.where(even, low, high)


def low_high(axis, first, second):
    even = is_even(axis)
    return jnp.where(even, second, first), jnp.where(even, first, second)


def slabs_kernel(
    disp, lame, shear, vel, mass, faces, five, first, second, vel_out, mass_out, faces_out
):
    vel_out[...] = vel[...]
    mass_out[...] = mass[...]
    faces_out[...] = faces[...]
    for c in range(5):
        block = disp[c] if c < 3 else (lame[...] if c == 3 else shear[...])
        five[c] = block
        store_faces("len", first, second, c, block[0], block[NI - 1])


def widen_kernel(block, x_first, x_second, out):
    for c in range(block.shape[0]):
        out[c, 0], out[c, NI + 1] = low_high("len", x_first[c], x_second[c])
        for i in range(NI):
            out[c, i + 1] = block[c, i]


def face_rows(planes, j):
    rows = [x[j : j + 1, :] for x in planes]
    return jnp.concatenate(rows + [jnp.zeros((8 - len(rows), NK), F32)], axis=0)


def rim_kernel(near, other, first, second):
    for half, source in enumerate((near, other)):
        for c in range(source.shape[0]):
            planes = [source[c, i] for i in range(NI + 2)]
            low, high = face_rows(planes, 0), face_rows(planes, NJ - 1)
            store_faces("wid", first, second, half * source.shape[0] + c, low, high)


def ring_kernel(block, x_first, x_second, first, second):
    for c in range(block.shape[0]):
        x_low, x_high = low_high("len", x_first[c], x_second[c])
        planes = [x_low] + [block[c, i] for i in range(NI)] + [x_high]
        store_faces("wid", first, second, c, face_rows(planes, 0), face_rows(planes, NJ - 1))


def put_planes(out, c, planes, first, second):
    low, high = low_high("wid", first, second)
    for i, plane in enumerate(planes):
        out[c, i, 1:9, :] = plane
        out[c, i, 0:1, :] = low[i : i + 1, :]
        out[c, i, 9:10, :] = high[i : i + 1, :]
        out[c, i, 10:16, :] = jnp.zeros((6, NK), F32)


def extend(source, first, second, half, out):
    for c in range(source.shape[0]):
        at = half * source.shape[0] + c
        put_planes(out, c, [source[c, i] for i in range(NI + 2)], first[at], second[at])


def extend_kernel(block, x_first, x_second, y_first, y_second, out):
    for c in range(block.shape[0]):
        x_low, x_high = low_high("len", x_first[c], x_second[c])
        planes = [x_low] + [block[c, i] for i in range(NI)] + [x_high]
        put_planes(out, c, planes, y_first[c], y_second[c])


def far_plane(near, other):
    lay = lax.axis_index("lay")
    lane = iota(near.shape, 2)
    edge = jnp.where(lay == 0, 0, NK - 1)
    shift = jnp.where(lay == 0, NK - 1, 1)
    return pltpu.roll(jnp.where(lane == edge, other, near), shift, 2)


def from_far(x):
    lay = lax.axis_index("lay")
    lane = iota(x.shape, 2)
    edge = jnp.where(lay == 0, 0, NK - 1)
    shift = jnp.where(lay == 0, 1, NK - 1)
    return jnp.where(lane == edge, 0.0, pltpu.roll(x, shift, 2))


def next_row(x):
    return pltpu.roll(x, x.shape[1] - 1, 1)


def element_moduli(near, other):
    total = near + far_plane(near, other)
    total = total + next_row(total)
    total = (total[0:5] + total[1:6]) * 0.125
    plane = iota(total.shape, 0)
    row = iota(total.shape, 1)
    at_len = lax.axis_index("len")
    at_wid = lax.axis_index("wid")
    outside = (plane == 0) & (at_len == 0)
    outside |= (plane == NI) & (at_len == lax.axis_size("len") - 1)
    outside |= (row == 0) & (at_wid == 0)
    outside |= (row == NJ) & (at_wid == lax.axis_size("wid") - 1)
    return jnp.where(outside, 0.0, total)


def internal_force(near_ref, other_ref, lame, shear):
    sigma = jnp.where(lax.axis_index("lay") == 0, 1.0, -1.0)
    grad = []
    means = []
    for c in range(3):
        near = near_ref[c]
        far = far_plane(near, other_ref[c])
        both = far + near
        diff = far - near
        both_next = next_row(both)
        sums = both + both_next
        cross = both_next - both
        tall = diff + next_row(diff)
        means.append((sums[0:5] + sums[1:6]) * 0.125)
        grad.append(
            [
                (sums[1:6] - sums[0:5]) * 0.25,
                (cross[0:5] + cross[1:6]) * 0.25,
                (tall[0:5] + tall[1:6]) * (0.25 * sigma),
            ]
        )
    pressure = lame * (grad[0][0] + grad[1][1] + grad[2][2])
    damping = HOURGLASS * shear
    damp_x = damping[0:4] + damping[1:5]
    damp_y = damp_x + next_row(damp_x)
    damp = (damp_y + from_far(damp_y))[:, 0:8]
    out = []
    for c in range(3):
        flux = []
        for j in range(3):
            stress = shear * (grad[c][j] + grad[j][c])
            if c == j:
                stress = stress + pressure
            flux.append(0.5 * damping * grad[c][j] - 0.25 * stress)
        lead = damping * means[c]
        depth = flux[2] * sigma
        lead_x = (lead[0:4] + lead[1:5]) + (flux[0][0:4] - flux[0][1:5])
        side_x = flux[1][0:4] + flux[1][1:5]
        depth_x = depth[0:4] + depth[1:5]
        lead_y = (lead_x + next_row(lead_x)) + (side_x - next_row(side_x))
        depth_y = depth_x + next_row(depth_x)
        force = (lead_y - depth_y) + from_far(lead_y + depth_y)
        out.append(force[:, 0:8] - near_ref[c, 1:5, 1:9, :] * damp)
    return out


def internal_first_kernel(near, other, y_low, y_high, out, moduli, here, there):
    extend(near, y_low, y_high, 0, here)
    extend(other, y_low, y_high, 1, there)
    lame = element_moduli(here[3], there[3])
    shear = element_moduli(here[4], there[4])
    moduli[0] = lame
    moduli[1] = shear
    for c, force in enumerate(internal_force(here, there, lame, shear)):
        out[c] = force


def column_to_row(column):
    size = column.shape[0]
    eye = iota((size, size), 0) == iota((size, size), 1)
    return jnp.sum(jnp.where(eye, column, 0.0), axis=0, keepdims=True)


def row_to_column(row):
    size = row.shape[1]
    eye = iota((size, size), 0) == iota((size, size), 1)
    return jnp.sum(jnp.where(eye, row, 0.0), axis=1, keepdims=True)


def request_kernel(
    u, slaves, gaps, chosen, owners, wanted, send, slot_of, at_slaves, slaves_out, gaps_out
):
    slaves_out[...] = slaves[...]
    gaps_out[...] = gaps[...]
    owner_row = owners[...].astype(F32)
    owner = row_to_column(owner_row)
    same = (owner == owner_row) & (iota((PAIRS, PAIRS), 1) < iota((PAIRS, PAIRS), 0))
    rank = jnp.max(jnp.where(same, 1.0, 0.0), axis=1, keepdims=True)
    slot = rank * GROUPS + owner
    slot_row = column_to_row(slot)
    slot_of[...] = jnp.where(slot == iota((PAIRS, SLOTS), 1).astype(F32), 1.0, 0.0)
    place = jnp.where(slot_row == iota((SLOTS, PAIRS), 0).astype(F32), 1.0, 0.0).astype(BF16)
    gather_nodes(u, slaves, at_slaves)
    values = [at_slaves[c] for c in range(3)]
    exact = jnp.concatenate(values + [gaps[...]], axis=1)
    moved = select_dot(place, exact)
    patch = jnp.broadcast_to(row_to_column(wanted[...].astype(F32) + 1.0), (PAIRS, PATCH))
    whole = jnp.concatenate([chosen[...].astype(F32), patch], axis=1).astype(BF16)
    moved_whole = jnp.dot(place, whole, preferred_element_type=F32)
    for t in range(CAP):
        part = slice(t * GROUPS, (t + 1) * GROUPS)
        for c in range(4):
            send[pl.ds(t * 4 + c, GROUPS, stride=12), :] = moved[part, c * 128 : (c + 1) * 128]
        for c in range(2):
            send[pl.ds(8 + t * 2 + c, GROUPS, stride=12), :] = moved_whole[
                part, c * 128 : (c + 1) * 128
            ]


def wanted_rows(arrived):
    patch = jnp.concatenate([every(arrived, 9, 12), every(arrived, 11, 12)], axis=0)
    cand = jnp.concatenate([every(arrived, 8, 12), every(arrived, 10, 12)], axis=0)
    at = (iota((SLOTS, PATCH), 1) % PATCHES + 1).astype(F32)
    onehot = jnp.where(patch == at, 1.0, 0.0).astype(BF16)
    return onehot, cand.astype(I32)


def table_kernel(u, faces, table, normals):
    table[...] = patch_table(u, faces[...], normals)


def reply_kernel(arrived, table, faces, send, face_row, face_lane):
    onehot, cand = wanted_rows(arrived)
    tiles = jnp.dot(onehot, table[...], preferred_element_type=F32)
    for c in range(4):
        picked = lane_pick(tiles[:, c * 128 : (c + 1) * 128], cand)
        for t in range(CAP):
            send[pl.ds(t * 4 + c, GROUPS, stride=8), :] = picked[t * GROUPS : (t + 1) * GROUPS]
    index = jnp.concatenate([faces[...] >> 7, faces[...] & 127], axis=1).astype(F32)
    index = jnp.concatenate(
        [index, jnp.zeros((PATCH - PATCHES, 2 * PATCH), F32)], axis=0
    ).astype(BF16)
    index = jnp.dot(onehot, index, preferred_element_type=F32)
    face_row[...] = lane_pick(index[:, 0:128], cand).astype(I32)
    face_lane[...] = lane_pick(index[:, 128:256], cand).astype(I32)


def owner_forces(values, gap_source, frames, stride, offset, frame_stride, frame_offset, scratch):
    for t in range(CAP):
        u = [every(values, t * offset + c, stride) for c in range(3)]
        gap = every(gap_source, t * 4 + 3, 12)
        frame = [every(frames, t * frame_offset[1] + frame_offset[0] + c, frame_stride) for c in range(4)]
        push = pair_push(u, frame[0:3], frame[3], gap)
        store_parts(scratch, 0, t * GROUPS, -0.25 * push)


def scatter_faces(row_ref, lane_ref, push_ref, size):
    row_at = iota((ROWS, PATCH), 0).astype(F32).astype(BF16)
    lane_at = iota((PATCH, PATCH), 0).astype(F32).astype(BF16)
    none = jnp.zeros((ROWS, PATCH), BF16)

    def body(i, acc):
        start = pl.multiple_of(i * size, size)
        rows = row_ref[pl.ds(start, size), :].astype(F32)
        lanes = lane_ref[pl.ds(start, size), :].astype(F32)
        parts = [push_ref[c, pl.ds(start, size), :] for c in range(2)]
        left = []
        right = []
        for q in range(size):
            here = jnp.concatenate([packed_row(rows, q)] * 2, axis=0) == row_at
            pieces = [
                jnp.where(here, jnp.concatenate([packed_row(part, q)] * 2, axis=0), none)
                for part in parts
            ]
            left.append(jnp.concatenate(pieces, axis=0))
            chosen = jnp.concatenate([packed_row(lanes, q)] * 8, axis=0) == lane_at
            right.append(jnp.where(chosen, jnp.ones_like(lane_at), jnp.zeros_like(lane_at)))
        left = jnp.concatenate(left, axis=1)
        right = jnp.concatenate(right, axis=1)
        return acc + lax.dot_general(
            left, right, (((1,), (1,)), ((), ())), preferred_element_type=F32
        )

    acc = lax.fori_loop(0, SLOTS // size, body, jnp.zeros((2 * ROWS, PATCH), F32))
    return acc[0:ROWS] + acc[ROWS : 2 * ROWS]


def face_contact(face_row, face_lane, normals, scratch):
    push = scatter_faces(face_row, face_lane, scratch, 128)
    out = []
    for c in range(3):
        x = jnp.where(push == 0.0, 0.0, push * normals[c])
        out.append(x + down_rows(x, 8) + down_rows(x, 9) + down_rows(x, 1))
    return out


def slave_contact(arrived, stride, offset, slot_of, at_slaves, gaps, slaves, scratch):
    onehot = slot_of[...].astype(BF16)
    slots = []
    for c in range(4):
        slots.append(
            jnp.concatenate(
                [every(arrived, t * offset[1] + offset[0] + c, stride) for t in range(CAP)], axis=0
            )
        )
    mine = select_dot(onehot, jnp.concatenate(slots, axis=1))
    frame = [mine[:, c * 128 : (c + 1) * 128] for c in range(4)]
    push = pair_push([at_slaves[c] for c in range(3)], frame[0:3], frame[3], gaps[...])
    for c in range(3):
        store_parts(scratch, c, 0, push * frame[c])

    def row_lane(start, size):
        nodes = slaves[pl.ds(start, size), :]
        return nodes >> 7, nodes & 127

    return scatter_nodes(PAIRS, row_lane, scratch)


def reaction_kernel(arrived, frames, face_row, face_lane, normals, out, scratch):
    owner_forces(arrived, arrived, frames, 12, 4, 8, (0, 4), scratch)
    for c, force in enumerate(face_contact(face_row, face_lane, normals, scratch)):
        out[c] = force


def advance(c, force, disp, vel, mass, new_disp, new_vel):
    moved = vel[c] + TIME_STEP * force / mass[...]
    new_vel[c] = moved
    place = disp[c] + TIME_STEP * moved
    new_disp[c] = place
    return place


def middle_kernel(
    arrived, slot_of, at_slaves, gaps, slaves, reaction, internal, disp, vel, mass,
    new_disp, new_vel, first, second, scratch,
):
    contact = slave_contact(arrived, 8, (0, 4), slot_of, at_slaves, gaps, slaves, scratch)
    for c in range(3):
        force = internal[c] + (contact[c] + reaction[c])
        place = advance(c, force, disp, vel, mass, new_disp, new_vel)
        store_faces("len", first, second, c, place[0:NJ], place[ROWS - NJ : ROWS])


def second_kernel(u, slaves, faces, slot_of, arrived, send, at_slaves, normals):
    gather_nodes(u, slaves, at_slaves)
    values = [at_slaves[c] for c in range(3)]
    place = slot_of[...].astype(BF16)
    high, mid, low = parts_3(jnp.concatenate(values, axis=1))
    dims = (((0,), (0,)), ((), ()))
    moved = lax.dot_general(place, low, dims, preferred_element_type=F32)
    moved = moved + lax.dot_general(place, mid, dims, preferred_element_type=F32)
    moved = moved + lax.dot_general(place, high, dims, preferred_element_type=F32)
    table = patch_table(u, faces[...], normals)
    onehot, cand = wanted_rows(arrived)
    tiles = jnp.dot(onehot, table, preferred_element_type=F32)
    for t in range(CAP):
        part = slice(t * GROUPS, (t + 1) * GROUPS)
        for c in range(3):
            send[pl.ds(t * 7 + c, GROUPS, stride=14), :] = moved[part, c * 128 : (c + 1) * 128]
    for c in range(4):
        picked = lane_pick(tiles[:, c * 128 : (c + 1) * 128], cand)
        for t in range(CAP):
            send[pl.ds(t * 7 + 3 + c, GROUPS, stride=14), :] = picked[
                t * GROUPS : (t + 1) * GROUPS
            ]


def contact_kernel(
    arrived, sent, first, face_row, face_lane, normals, slot_of, at_slaves, gaps, slaves, out,
    scratch, slave_scratch,
):
    owner_forces(arrived, first, sent, 14, 7, 14, (3, 7), scratch)
    reaction = face_contact(face_row, face_lane, normals, scratch)
    contact = slave_contact(arrived, 14, (3, 7), slot_of, at_slaves, gaps, slaves, slave_scratch)
    for c in range(3):
        out[c] = contact[c] + reaction[c]


def finish_kernel(near, other, moduli, contact, disp, vel, mass, new_disp, new_vel):
    for c, internal in enumerate(internal_force(near, other, moduli[0], moduli[1])):
        moved = vel[c] + TIME_STEP * (internal + contact[c]) / mass[...]
        new_vel[c] = moved
        new_disp[c] = disp[c] + TIME_STEP * moved


def f32(*shape):
    return pltpu.VMEM(shape, F32)


def i32(*shape):
    return pltpu.VMEM(shape, I32)


def plain(*shape):
    return jax.ShapeDtypeStruct(shape, F32)


def call(kernel, outs, *args, scratch=(), raw=0):
    local = pl.BlockSpec(memory_space=pltpu.VMEM)
    whole = pl.BlockSpec()
    inputs = [
        x if i < raw else pltpu.with_memory_space_constraint(x, pltpu.VMEM)
        for i, x in enumerate(args)
    ]
    return pl.pallas_call(
        kernel,
        out_shape=outs,
        in_specs=[whole if i < raw else local for i in range(len(args))],
        out_specs=jax.tree.map(
            lambda x: whole if isinstance(x, jax.ShapeDtypeStruct) else local, outs
        ),
        scratch_shapes=[pltpu.VMEM(s, F32) for s in scratch],
    )(*inputs)


def swap_pair(first, second, axis):
    count = lax.axis_size(axis)
    mate = [(i, i ^ 1) for i in range(count)]
    other = [(i, (i - 1 if i % 2 == 0 else i + 1) % count) for i in range(count)]
    return lax.ppermute(first, axis, mate), lax.ppermute(second, axis, other)


def surroundings(block, low, high):
    parts = block.shape[0]
    x_low, x_high = swap_pair(low, high, "len")
    near = call(widen_kernel, f32(parts, NI + 2, NJ, NK), block, x_low, x_high)
    other = lax.ppermute(near, "lay", [(0, 1), (1, 0)])
    low, high = call(rim_kernel, (f32(2 * parts, 8, NK), f32(2 * parts, 8, NK)), near, other)
    y_low, y_high = swap_pair(low, high, "wid")
    return near, other, y_low, y_high


def extended(block, low, high):
    x_low, x_high = swap_pair(low, high, "len")
    low, high = call(ring_kernel, (f32(3, 8, NK), f32(3, 8, NK)), block, x_low, x_high)
    y_low, y_high = swap_pair(low, high, "wid")
    near = call(extend_kernel, f32(3, NI + 2, 16, NK), block, x_low, x_high, y_low, y_high)
    other = lax.ppermute(near, "lay", [(0, 1), (1, 0)])
    return near, other


def exchange(buffer):
    chunk = buffer.reshape(GROUPS, 1, -1)
    out = lax.all_to_all(chunk, ("len", "wid"), split_axis=0, concat_axis=0, tiled=True)
    return out.reshape(buffer.shape)


def program(
    displacement, velocity, lame_first, shear_modulus, nodal_mass, slave_nodes, initial_gap,
    candidate, pair_owner, pair_patch, master_faces,
):
    slaves = slave_nodes.reshape(PAIRS, PATCH)
    gaps = initial_gap.reshape(PAIRS, PATCH)
    chosen = candidate.reshape(PAIRS, PATCH)
    owners = pair_owner.reshape(1, PAIRS)
    wanted = pair_patch.reshape(1, PAIRS)
    faces = master_faces.reshape(PATCHES, PATCH)
    u = displacement.reshape(3, ROWS, NK)
    v = velocity.reshape(3, ROWS, NK)
    mass = nodal_mass.reshape(ROWS, NK)
    five, low, high, v, mass, faces = call(
        slabs_kernel,
        (
            f32(5, NI, NJ, NK), f32(5, NJ, NK), f32(5, NJ, NK), f32(3, ROWS, NK), f32(ROWS, NK),
            i32(PATCHES, PATCH),
        ),
        displacement, lame_first, shear_modulus, v, mass, faces, raw=6,
    )
    around = surroundings(five, low, high)
    send, slot_of, at_slaves, slaves, gaps = call(
        request_kernel,
        (
            plain(GROUPS * 12, PATCH), f32(PAIRS, SLOTS), f32(3, PAIRS, PATCH),
            i32(PAIRS, PATCH), f32(PAIRS, PATCH),
        ),
        u, slaves, gaps, chosen, owners, wanted, raw=6,
    )
    first = exchange(send)
    table, normals = call(
        table_kernel, (pltpu.VMEM((128, 512), BF16), f32(3, ROWS, NK)), u, faces
    )
    reply, face_row, face_lane = call(
        reply_kernel,
        (plain(GROUPS * 8, PATCH), i32(SLOTS, PATCH), i32(SLOTS, PATCH)),
        first, table, faces,
    )
    arrived = exchange(reply)
    reaction = call(
        reaction_kernel, f32(3, ROWS, NK), first, reply, face_row, face_lane, normals,
        scratch=[(2, SLOTS, PATCH)],
    )
    internal, moduli = call(
        internal_first_kernel, (f32(3, NI, NJ, NK), f32(2, 5, 16, NK)), *around,
        scratch=[(5, NI + 2, 16, NK)] * 2,
    )
    u, v, low, high = call(
        middle_kernel,
        (f32(3, ROWS, NK), f32(3, ROWS, NK), f32(3, NJ, NK), f32(3, NJ, NK)),
        arrived, slot_of, at_slaves, gaps, slaves, reaction, internal.reshape(3, ROWS, NK),
        u, v, mass,
        scratch=[(6, PAIRS, PATCH)],
    )
    near, other = extended(u.reshape(3, NI, NJ, NK), low, high)
    sent, at_slaves, next_normals = call(
        second_kernel,
        (plain(GROUPS * 14, PATCH), f32(3, PAIRS, PATCH), f32(3, ROWS, NK)),
        u, slaves, faces, slot_of, first,
    )
    arrived = exchange(sent)
    contact = call(
        contact_kernel, f32(3, ROWS, NK),
        arrived, sent, first, face_row, face_lane, next_normals, slot_of, at_slaves, gaps, slaves,
        scratch=[(2, SLOTS, PATCH), (6, PAIRS, PATCH)],
    )
    block = (3, NI, NJ, NK)
    u, v = call(
        finish_kernel, (plain(*block), plain(*block)),
        near, other, moduli, contact.reshape(block), u.reshape(block), v.reshape(block),
        mass.reshape(NI, NJ, NK),
    )
    return u.reshape(displacement.shape), v.reshape(velocity.shape)


def solution(mesh):
    nodal = P("len", "wid", "lay")
    vector = P(None, "len", "wid", "lay")
    in_specs = (
        vector, vector, nodal, nodal, nodal,
        P("len", "wid", "lay", None, None),
        P("len", "wid", "lay", None, None),
        P("len", "wid", "lay", None, None),
        P("len", "wid", "lay", None, None),
        P("len", "wid", "lay", None),
        P("len", "wid", "lay", None, None),
    )
    return jax.shard_map(
        program, mesh=mesh, in_specs=in_specs, out_specs=(vector, vector), check_vma=False
    )
```

```python
import jax
import jax.numpy as jnp
from jax import lax
from jax.experimental import pallas as pl
from jax.experimental.pallas import tpu as pltpu
from jax.sharding import PartitionSpec as P


PENALTY = 4.0
HOURGLASS = 0.3
TIME_STEP = 0.25

NI, NJ, NK = 4, 8, 128
ROWS = NI * NJ
PAIRS = 64
PATCH = 128
PATCHES = 32
GROUPS = 64
CAP = 2
SLOTS = GROUPS * CAP
F32 = jnp.float32
BF16 = jnp.bfloat16
I32 = jnp.int32


def iota(shape, axis):
    return lax.broadcasted_iota(I32, shape, axis)


def lane_pick(values, index):
    return jnp.take_along_axis(values, index, axis=1, mode="promise_in_bounds")


def parts_3(x):
    high = x.astype(BF16)
    rest = x - high.astype(F32)
    mid = rest.astype(BF16)
    low = (rest - mid.astype(F32)).astype(BF16)
    return high, mid, low


def select_dot(onehot, x):
    high, mid, low = parts_3(x)
    return jnp.dot(
        jnp.concatenate([onehot] * 3, axis=1),
        jnp.concatenate([low, mid, high], axis=0),
        preferred_element_type=F32,
    )


def gather_flat(u_ref, slaves, out_ref):
    for start in range(0, PAIRS, 8):
        nodes = slaves[pl.ds(start, 8), :]
        row = nodes >> 7
        lane = nodes & 127
        out = [jnp.zeros((8, PATCH), F32) for _ in range(3)]
        for r in range(ROWS):
            here = row == r
            for c in range(3):
                source = jnp.broadcast_to(u_ref[c, r : r + 1, :], (8, PATCH))
                out[c] = jnp.where(here, lane_pick(source, lane), out[c])
        for c in range(3):
            out_ref[c, pl.ds(start, 8), :] = out[c]


def up(x, amount):
    return pltpu.roll(x, x.shape[0] - amount, 0)


def patch_table(u_ref, faces, normals):
    frames = []
    one = [u_ref[c] for c in range(3)]
    two = [up(x, 8) for x in one]
    three = [up(x, 9) for x in one]
    four = [up(x, 1) for x in one]
    centroid = [(one[c] + two[c] + three[c] + four[c]) * 0.25 for c in range(3)]
    da = [three[0] - one[0] + 1.0, three[1] - one[1] + 1.0, three[2] - one[2]]
    db = [four[0] - two[0] - 1.0, four[1] - two[1] + 1.0, four[2] - two[2]]
    normal = [
        da[1] * db[2] - da[2] * db[1],
        da[2] * db[0] - da[0] * db[2],
        da[0] * db[1] - da[1] * db[0],
    ]
    length = jnp.sqrt(normal[0] * normal[0] + normal[1] * normal[1] + normal[2] * normal[2])
    normal = [x / length for x in normal]
    offset = centroid[0] * normal[0] + centroid[1] * normal[1] + centroid[2] * normal[2]
    frames = normal + [offset]
    for c in range(3):
        normals[c] = normal[c]
    out = [[] for _ in range(4)]
    for start in range(0, PATCHES, 8):
        row = faces[start : start + 8] >> 7
        lane = faces[start : start + 8] & 127
        best = [jnp.zeros((8, PATCH), F32) for _ in range(4)]
        for r in range((NI - 1) * NJ):
            if r % NJ == NJ - 1:
                continue
            here = row == r
            for c in range(4):
                source = jnp.broadcast_to(frames[c][r : r + 1, :], (8, PATCH))
                best[c] = jnp.where(here, lane_pick(source, lane), best[c])
        for c in range(4):
            out[c].append(best[c])
    out = [jnp.concatenate(x, axis=0) for x in out]
    table = jnp.concatenate(out, axis=1)
    high, mid, low = parts_3(table)
    return jnp.concatenate([high, mid, low, jnp.zeros_like(high)], axis=0)


def packed_row(x, q):
    return jnp.broadcast_to(x[q : q + 1, :], (16, PATCH)).astype(BF16)


def scatter_nodes(count, row_lane, forces_ref):
    pieces_count = forces_ref.shape[0]
    parts_count = pieces_count // 2
    size = 64
    row_at = iota((ROWS, PATCH), 0).astype(F32).astype(BF16)
    lane_at = iota((PATCH, PATCH), 0).astype(F32).astype(BF16)
    none = jnp.zeros((ROWS, PATCH), BF16)

    def body(i, acc):
        start = pl.multiple_of(i * size, size)
        rows, lanes = row_lane(start, size)
        rows = rows.astype(F32)
        lanes = lanes.astype(F32)
        parts = [forces_ref[c, pl.ds(start, size), :] for c in range(pieces_count)]
        left = []
        right = []
        for q in range(size):
            here = jnp.concatenate([packed_row(rows, q)] * 2, axis=0) == row_at
            pieces = [
                jnp.where(here, jnp.concatenate([packed_row(part, q)] * 2, axis=0), none)
                for part in parts
            ]
            left.append(jnp.concatenate(pieces, axis=0))
            chosen = jnp.concatenate([packed_row(lanes, q)] * 8, axis=0) == lane_at
            right.append(jnp.where(chosen, jnp.ones_like(lane_at), jnp.zeros_like(lane_at)))
        left = jnp.concatenate(left, axis=1)
        right = jnp.concatenate(right, axis=1)
        return acc + lax.dot_general(
            left, right, (((1,), (1,)), ((), ())), preferred_element_type=F32
        )

    acc = lax.fori_loop(0, count // size, body, jnp.zeros((pieces_count * ROWS, PATCH), F32))
    acc = acc[0 : parts_count * ROWS] + acc[parts_count * ROWS : pieces_count * ROWS]
    return [acc[c * ROWS : (c + 1) * ROWS] for c in range(parts_count)]


def store_parts(forces_ref, c, start, force):
    high = force.astype(BF16).astype(F32)
    forces_ref[c, start : start + force.shape[0], :] = high
    low = c + forces_ref.shape[0] // 2
    forces_ref[low, start : start + force.shape[0], :] = force - high


def down_rows(x, amount):
    moved = pltpu.roll(x, amount, 0)
    return jnp.where(iota(x.shape, 0) >= amount, moved, 0.0)


def pair_push(u, normal, offset, gap):
    now = gap + (u[0] * normal[0] + u[1] * normal[1] + u[2] * normal[2]) - offset
    return -PENALTY * jnp.minimum(now, 0.0)


def every(ref, start, stride):
    return ref[pl.ds(start, GROUPS, stride=stride), :]


def is_even(axis):
    return lax.axis_index(axis) % 2 == 0


def store_faces(axis, first, second, at, low, high):
    even = is_even(axis)
    first[at] = jnp.where(even, high, low)
    second[at] = jnp.where(even, low, high)


def low_high(axis, first, second):
    even = is_even(axis)
    return jnp.where(even, second, first), jnp.where(even, first, second)


def slabs_kernel(
    disp, lame, shear, vel, mass, faces, five, first, second, vel_out, mass_out, faces_out
):
    vel_out[...] = vel[...]
    mass_out[...] = mass[...]
    faces_out[...] = faces[...]
    for c in range(5):
        block = disp[c] if c < 3 else (lame[...] if c == 3 else shear[...])
        five[c] = block
        store_faces("len", first, second, c, block[0], block[NI - 1])


def widen_kernel(block, x_first, x_second, out):
    for c in range(block.shape[0]):
        out[c, 0], out[c, NI + 1] = low_high("len", x_first[c], x_second[c])
        for i in range(NI):
            out[c, i + 1] = block[c, i]


def face_rows(planes, j):
    rows = [x[j : j + 1, :] for x in planes]
    return jnp.concatenate(rows + [jnp.zeros((8 - len(rows), NK), F32)], axis=0)


def rim_kernel(near, other, first, second):
    for half, source in enumerate((near, other)):
        for c in range(source.shape[0]):
            planes = [source[c, i] for i in range(NI + 2)]
            low, high = face_rows(planes, 0), face_rows(planes, NJ - 1)
            store_faces("wid", first, second, half * source.shape[0] + c, low, high)


def ring_kernel(block, x_first, x_second, first, second):
    for c in range(block.shape[0]):
        x_low, x_high = low_high("len", x_first[c], x_second[c])
        planes = [x_low] + [block[c, i] for i in range(NI)] + [x_high]
        store_faces("wid", first, second, c, face_rows(planes, 0), face_rows(planes, NJ - 1))


def put_planes(out, c, planes, first, second):
    low, high = low_high("wid", first, second)
    for i, plane in enumerate(planes):
        out[c, i, 1:9, :] = plane
        out[c, i, 0:1, :] = low[i : i + 1, :]
        out[c, i, 9:10, :] = high[i : i + 1, :]
        out[c, i, 10:16, :] = jnp.zeros((6, NK), F32)


def extend(source, first, second, half, out):
    for c in range(source.shape[0]):
        at = half * source.shape[0] + c
        put_planes(out, c, [source[c, i] for i in range(NI + 2)], first[at], second[at])


def extend_kernel(block, x_first, x_second, y_first, y_second, out):
    for c in range(block.shape[0]):
        x_low, x_high = low_high("len", x_first[c], x_second[c])
        planes = [x_low] + [block[c, i] for i in range(NI)] + [x_high]
        put_planes(out, c, planes, y_first[c], y_second[c])


def far_plane(near, other):
    lay = lax.axis_index("lay")
    lane = iota(near.shape, 2)
    edge = jnp.where(lay == 0, 0, NK - 1)
    shift = jnp.where(lay == 0, NK - 1, 1)
    return pltpu.roll(jnp.where(lane == edge, other, near), shift, 2)


def from_far(x):
    lay = lax.axis_index("lay")
    lane = iota(x.shape, 2)
    edge = jnp.where(lay == 0, 0, NK - 1)
    shift = jnp.where(lay == 0, 1, NK - 1)
    return jnp.where(lane == edge, 0.0, pltpu.roll(x, shift, 2))


def next_row(x):
    return pltpu.roll(x, x.shape[1] - 1, 1)


def element_moduli(near, other):
    total = near + far_plane(near, other)
    total = total + next_row(total)
    total = (total[0:5] + total[1:6]) * 0.125
    plane = iota(total.shape, 0)
    row = iota(total.shape, 1)
    at_len = lax.axis_index("len")
    at_wid = lax.axis_index("wid")
    outside = (plane == 0) & (at_len == 0)
    outside |= (plane == NI) & (at_len == lax.axis_size("len") - 1)
    outside |= (row == 0) & (at_wid == 0)
    outside |= (row == NJ) & (at_wid == lax.axis_size("wid") - 1)
    return jnp.where(outside, 0.0, total)


def internal_force(near_ref, other_ref, lame, shear):
    sigma = jnp.where(lax.axis_index("lay") == 0, 1.0, -1.0)
    grad = []
    means = []
    for c in range(3):
        near = near_ref[c]
        far = far_plane(near, other_ref[c])
        both = far + near
        diff = far - near
        both_next = next_row(both)
        sums = both + both_next
        cross = both_next - both
        tall = diff + next_row(diff)
        means.append((sums[0:5] + sums[1:6]) * 0.125)
        grad.append(
            [
                (sums[1:6] - sums[0:5]) * 0.25,
                (cross[0:5] + cross[1:6]) * 0.25,
                (tall[0:5] + tall[1:6]) * (0.25 * sigma),
            ]
        )
    pressure = lame * (grad[0][0] + grad[1][1] + grad[2][2])
    damping = HOURGLASS * shear
    damp_x = damping[0:4] + damping[1:5]
    damp_y = damp_x + next_row(damp_x)
    damp = (damp_y + from_far(damp_y))[:, 0:8]
    out = []
    for c in range(3):
        flux = []
        for j in range(3):
            stress = shear * (grad[c][j] + grad[j][c])
            if c == j:
                stress = stress + pressure
            flux.append(0.5 * damping * grad[c][j] - 0.25 * stress)
        lead = damping * means[c]
        depth = flux[2] * sigma
        lead_x = (lead[0:4] + lead[1:5]) + (flux[0][0:4] - flux[0][1:5])
        side_x = flux[1][0:4] + flux[1][1:5]
        depth_x = depth[0:4] + depth[1:5]
        lead_y = (lead_x + next_row(lead_x)) + (side_x - next_row(side_x))
        depth_y = depth_x + next_row(depth_x)
        force = (lead_y - depth_y) + from_far(lead_y + depth_y)
        out.append(force[:, 0:8] - near_ref[c, 1:5, 1:9, :] * damp)
    return out


def internal_first_kernel(near, other, y_low, y_high, out, moduli, here, there):
    extend(near, y_low, y_high, 0, here)
    extend(other, y_low, y_high, 1, there)
    lame = element_moduli(here[3], there[3])
    shear = element_moduli(here[4], there[4])
    moduli[0] = lame
    moduli[1] = shear
    for c, force in enumerate(internal_force(here, there, lame, shear)):
        out[c] = force


def column_to_row(column):
    size = column.shape[0]
    eye = iota((size, size), 0) == iota((size, size), 1)
    return jnp.sum(jnp.where(eye, column, 0.0), axis=0, keepdims=True)


def row_to_column(row):
    size = row.shape[1]
    eye = iota((size, size), 0) == iota((size, size), 1)
    return jnp.sum(jnp.where(eye, row, 0.0), axis=1, keepdims=True)


def request_kernel(
    u, slaves, gaps, chosen, owners, wanted, send, slot_of, place_out, at_slaves, slaves_out, gaps_out
):
    slaves_out[...] = slaves[...]
    gaps_out[...] = gaps[...]
    owner_row = owners[...].astype(F32)
    owner = row_to_column(owner_row)
    same = (owner == owner_row) & (iota((PAIRS, PAIRS), 1) < iota((PAIRS, PAIRS), 0))
    rank = jnp.max(jnp.where(same, 1.0, 0.0), axis=1, keepdims=True)
    slot = rank * GROUPS + owner
    slot_row = column_to_row(slot)
    slot_of[...] = jnp.where(slot == iota((PAIRS, SLOTS), 1).astype(F32), 1.0, 0.0)
    place = jnp.where(slot_row == iota((SLOTS, PAIRS), 0).astype(F32), 1.0, 0.0).astype(BF16)
    place_out[...] = place
    gather_flat(u, slaves, at_slaves)
    values = [at_slaves[c] for c in range(3)]
    exact = jnp.concatenate(values + [gaps[...]], axis=1)
    moved = select_dot(place, exact)
    patch = jnp.broadcast_to(row_to_column(wanted[...].astype(F32) + 1.0), (PAIRS, PATCH))
    whole = jnp.concatenate([chosen[...].astype(F32), patch], axis=1).astype(BF16)
    moved_whole = jnp.dot(place, whole, preferred_element_type=F32)
    for t in range(CAP):
        part = slice(t * GROUPS, (t + 1) * GROUPS)
        for c in range(4):
            send[pl.ds(t * 4 + c, GROUPS, stride=12), :] = moved[part, c * 128 : (c + 1) * 128]
        for c in range(2):
            send[pl.ds(8 + t * 2 + c, GROUPS, stride=12), :] = moved_whole[
                part, c * 128 : (c + 1) * 128
            ]


def wanted_rows(arrived):
    patch = jnp.concatenate([every(arrived, 9, 12), every(arrived, 11, 12)], axis=0)
    cand = jnp.concatenate([every(arrived, 8, 12), every(arrived, 10, 12)], axis=0)
    at = (iota((SLOTS, PATCH), 1) % PATCHES + 1).astype(F32)
    onehot = jnp.where(patch == at, 1.0, 0.0).astype(BF16)
    return onehot, cand.astype(I32)


def table_kernel(u, faces, table, normals):
    table[...] = patch_table(u, faces[...], normals)


def reply_kernel(arrived, table, faces, send, face_row, face_lane, patch_of, cand_of):
    onehot, cand = wanted_rows(arrived)
    patch_of[...] = onehot
    cand_of[...] = cand
    tiles = jnp.dot(onehot, table[...], preferred_element_type=F32)
    for c in range(4):
        picked = lane_pick(tiles[:, c * 128 : (c + 1) * 128], cand)
        for t in range(CAP):
            send[pl.ds(t * 4 + c, GROUPS, stride=8), :] = picked[t * GROUPS : (t + 1) * GROUPS]
    index = jnp.concatenate([faces[...] >> 7, faces[...] & 127], axis=1).astype(F32)
    index = jnp.concatenate(
        [index, jnp.zeros((PATCH - PATCHES, 2 * PATCH), F32)], axis=0
    ).astype(BF16)
    index = jnp.dot(onehot, index, preferred_element_type=F32)
    face_row[...] = lane_pick(index[:, 0:128], cand).astype(I32)
    face_lane[...] = lane_pick(index[:, 128:256], cand).astype(I32)


def owner_forces(values, gap_source, frames, stride, offset, frame_stride, frame_offset, scratch):
    for t in range(CAP):
        u = [every(values, t * offset + c, stride) for c in range(3)]
        gap = every(gap_source, t * 4 + 3, 12)
        frame = [every(frames, t * frame_offset[1] + frame_offset[0] + c, frame_stride) for c in range(4)]
        push = pair_push(u, frame[0:3], frame[3], gap)
        store_parts(scratch, 0, t * GROUPS, -0.25 * push)


def scatter_faces(row_ref, lane_ref, push_ref, size):
    row_at = iota((ROWS, PATCH), 0).astype(F32).astype(BF16)
    lane_at = iota((PATCH, PATCH), 0).astype(F32).astype(BF16)
    none = jnp.zeros((ROWS, PATCH), BF16)

    def body(i, acc):
        start = pl.multiple_of(i * size, size)
        rows = row_ref[pl.ds(start, size), :].astype(F32)
        lanes = lane_ref[pl.ds(start, size), :].astype(F32)
        parts = [push_ref[c, pl.ds(start, size), :] for c in range(2)]
        left = []
        right = []
        for q in range(size):
            here = jnp.concatenate([packed_row(rows, q)] * 2, axis=0) == row_at
            pieces = [
                jnp.where(here, jnp.concatenate([packed_row(part, q)] * 2, axis=0), none)
                for part in parts
            ]
            left.append(jnp.concatenate(pieces, axis=0))
            chosen = jnp.concatenate([packed_row(lanes, q)] * 8, axis=0) == lane_at
            right.append(jnp.where(chosen, jnp.ones_like(lane_at), jnp.zeros_like(lane_at)))
        left = jnp.concatenate(left, axis=1)
        right = jnp.concatenate(right, axis=1)
        return acc + lax.dot_general(
            left, right, (((1,), (1,)), ((), ())), preferred_element_type=F32
        )

    acc = lax.fori_loop(0, SLOTS // size, body, jnp.zeros((2 * ROWS, PATCH), F32))
    return acc[0:ROWS] + acc[ROWS : 2 * ROWS]


def face_contact(face_row, face_lane, normals, scratch):
    push = scatter_faces(face_row, face_lane, scratch, 128)
    out = []
    for c in range(3):
        x = jnp.where(push == 0.0, 0.0, push * normals[c])
        out.append(x + down_rows(x, 8) + down_rows(x, 9) + down_rows(x, 1))
    return out


def slave_contact(arrived, stride, offset, slot_of, at_slaves, gaps, slaves, scratch):
    onehot = slot_of[...].astype(BF16)
    slots = []
    for c in range(4):
        slots.append(
            jnp.concatenate(
                [every(arrived, t * offset[1] + offset[0] + c, stride) for t in range(CAP)], axis=0
            )
        )
    mine = select_dot(onehot, jnp.concatenate(slots, axis=1))
    frame = [mine[:, c * 128 : (c + 1) * 128] for c in range(4)]
    push = pair_push([at_slaves[c] for c in range(3)], frame[0:3], frame[3], gaps[...])
    for c in range(3):
        store_parts(scratch, c, 0, push * frame[c])

    def row_lane(start, size):
        nodes = slaves[pl.ds(start, size), :]
        return nodes >> 7, nodes & 127

    return scatter_nodes(PAIRS, row_lane, scratch)


def reaction_kernel(arrived, frames, face_row, face_lane, normals, out, scratch):
    owner_forces(arrived, arrived, frames, 12, 4, 8, (0, 4), scratch)
    for c, force in enumerate(face_contact(face_row, face_lane, normals, scratch)):
        out[c] = force


def advance(c, force, disp, vel, mass, new_disp, new_vel):
    moved = vel[c] + TIME_STEP * force / mass[...]
    new_vel[c] = moved
    place = disp[c] + TIME_STEP * moved
    new_disp[c] = place
    return place


def middle_kernel(
    arrived, slot_of, at_slaves, gaps, slaves, reaction, internal, disp, vel, mass,
    new_disp, new_vel, first, second, scratch,
):
    contact = slave_contact(arrived, 8, (0, 4), slot_of, at_slaves, gaps, slaves, scratch)
    for c in range(3):
        force = internal[c] + (contact[c] + reaction[c])
        place = advance(c, force, disp, vel, mass, new_disp, new_vel)
        store_faces("len", first, second, c, place[0:NJ], place[ROWS - NJ : ROWS])


def second_kernel(u, slaves, faces, place, patch_of, cand_of, send, at_slaves, normals):
    gather_flat(u, slaves, at_slaves)
    values = [at_slaves[c] for c in range(3)]
    moved = select_dot(place[...], jnp.concatenate(values, axis=1))
    table = patch_table(u, faces[...], normals)
    cand = cand_of[...]
    tiles = jnp.dot(patch_of[...], table, preferred_element_type=F32)
    for t in range(CAP):
        part = slice(t * GROUPS, (t + 1) * GROUPS)
        for c in range(3):
            send[pl.ds(t * 7 + c, GROUPS, stride=14), :] = moved[part, c * 128 : (c + 1) * 128]
    for c in range(4):
        picked = lane_pick(tiles[:, c * 128 : (c + 1) * 128], cand)
        for t in range(CAP):
            send[pl.ds(t * 7 + 3 + c, GROUPS, stride=14), :] = picked[
                t * GROUPS : (t + 1) * GROUPS
            ]


def contact_kernel(
    arrived, sent, first, face_row, face_lane, normals, slot_of, at_slaves, gaps, slaves, out,
    scratch, slave_scratch,
):
    owner_forces(arrived, first, sent, 14, 7, 14, (3, 7), scratch)
    reaction = face_contact(face_row, face_lane, normals, scratch)
    contact = slave_contact(arrived, 14, (3, 7), slot_of, at_slaves, gaps, slaves, slave_scratch)
    for c in range(3):
        out[c] = contact[c] + reaction[c]


def finish_kernel(near, other, moduli, contact, disp, vel, mass, new_disp, new_vel):
    for c, internal in enumerate(internal_force(near, other, moduli[0], moduli[1])):
        moved = vel[c] + TIME_STEP * (internal + contact[c]) / mass[...]
        new_vel[c] = moved
        new_disp[c] = disp[c] + TIME_STEP * moved


def f32(*shape):
    return pltpu.VMEM(shape, F32)


def i32(*shape):
    return pltpu.VMEM(shape, I32)


def plain(*shape):
    return jax.ShapeDtypeStruct(shape, F32)


def call(kernel, outs, *args, scratch=(), raw=0):
    local = pl.BlockSpec(memory_space=pltpu.VMEM)
    whole = pl.BlockSpec()
    inputs = [
        x if i < raw else pltpu.with_memory_space_constraint(x, pltpu.VMEM)
        for i, x in enumerate(args)
    ]
    return pl.pallas_call(
        kernel,
        out_shape=outs,
        in_specs=[whole if i < raw else local for i in range(len(args))],
        out_specs=jax.tree.map(
            lambda x: whole if isinstance(x, jax.ShapeDtypeStruct) else local, outs
        ),
        scratch_shapes=[pltpu.VMEM(s, F32) for s in scratch],
    )(*inputs)


def swap_pair(first, second, axis):
    count = lax.axis_size(axis)
    mate = [(i, i ^ 1) for i in range(count)]
    other = [(i, (i - 1 if i % 2 == 0 else i + 1) % count) for i in range(count)]
    return lax.ppermute(first, axis, mate), lax.ppermute(second, axis, other)


def surroundings(block, low, high):
    parts = block.shape[0]
    x_low, x_high = swap_pair(low, high, "len")
    near = call(widen_kernel, f32(parts, NI + 2, NJ, NK), block, x_low, x_high)
    other = lax.ppermute(near, "lay", [(0, 1), (1, 0)])
    low, high = call(rim_kernel, (f32(2 * parts, 8, NK), f32(2 * parts, 8, NK)), near, other)
    y_low, y_high = swap_pair(low, high, "wid")
    return near, other, y_low, y_high


def extended(block, low, high):
    x_low, x_high = swap_pair(low, high, "len")
    low, high = call(ring_kernel, (f32(3, 8, NK), f32(3, 8, NK)), block, x_low, x_high)
    y_low, y_high = swap_pair(low, high, "wid")
    near = call(extend_kernel, f32(3, NI + 2, 16, NK), block, x_low, x_high, y_low, y_high)
    other = lax.ppermute(near, "lay", [(0, 1), (1, 0)])
    return near, other


def exchange(buffer):
    chunk = buffer.reshape(GROUPS, 1, -1)
    out = lax.all_to_all(chunk, ("len", "wid"), split_axis=0, concat_axis=0, tiled=True)
    return out.reshape(buffer.shape)


def program(
    displacement, velocity, lame_first, shear_modulus, nodal_mass, slave_nodes, initial_gap,
    candidate, pair_owner, pair_patch, master_faces,
):
    slaves = slave_nodes.reshape(PAIRS, PATCH)
    gaps = initial_gap.reshape(PAIRS, PATCH)
    chosen = candidate.reshape(PAIRS, PATCH)
    owners = pair_owner.reshape(1, PAIRS)
    wanted = pair_patch.reshape(1, PAIRS)
    faces = master_faces.reshape(PATCHES, PATCH)
    u = displacement.reshape(3, ROWS, NK)
    v = velocity.reshape(3, ROWS, NK)
    mass = nodal_mass.reshape(ROWS, NK)
    five, low, high, v, mass, faces = call(
        slabs_kernel,
        (
            f32(5, NI, NJ, NK), f32(5, NJ, NK), f32(5, NJ, NK), f32(3, ROWS, NK), f32(ROWS, NK),
            i32(PATCHES, PATCH),
        ),
        displacement, lame_first, shear_modulus, v, mass, faces, raw=6,
    )
    around = surroundings(five, low, high)
    send, slot_of, place, at_slaves, slaves, gaps = call(
        request_kernel,
        (
            plain(GROUPS * 12, PATCH), f32(PAIRS, SLOTS), pltpu.VMEM((SLOTS, PAIRS), BF16),
            f32(3, PAIRS, PATCH),
            i32(PAIRS, PATCH), f32(PAIRS, PATCH),
        ),
        u, slaves, gaps, chosen, owners, wanted, raw=6,
    )
    first = exchange(send)
    table, normals = call(
        table_kernel, (pltpu.VMEM((128, 512), BF16), f32(3, ROWS, NK)), u, faces
    )
    reply, face_row, face_lane, patch_of, cand_of = call(
        reply_kernel,
        (
            plain(GROUPS * 8, PATCH), i32(SLOTS, PATCH), i32(SLOTS, PATCH),
            pltpu.VMEM((SLOTS, PATCH), BF16), i32(SLOTS, PATCH),
        ),
        first, table, faces,
    )
    arrived = exchange(reply)
    reaction = call(
        reaction_kernel, f32(3, ROWS, NK), first, reply, face_row, face_lane, normals,
        scratch=[(2, SLOTS, PATCH)],
    )
    internal, moduli = call(
        internal_first_kernel, (f32(3, NI, NJ, NK), f32(2, 5, 16, NK)), *around,
        scratch=[(5, NI + 2, 16, NK)] * 2,
    )
    u, v, low, high = call(
        middle_kernel,
        (f32(3, ROWS, NK), f32(3, ROWS, NK), f32(3, NJ, NK), f32(3, NJ, NK)),
        arrived, slot_of, at_slaves, gaps, slaves, reaction, internal.reshape(3, ROWS, NK),
        u, v, mass,
        scratch=[(6, PAIRS, PATCH)],
    )
    near, other = extended(u.reshape(3, NI, NJ, NK), low, high)
    sent, at_slaves, next_normals = call(
        second_kernel,
        (plain(GROUPS * 14, PATCH), f32(3, PAIRS, PATCH), f32(3, ROWS, NK)),
        u, slaves, faces, place, patch_of, cand_of,
    )
    arrived = exchange(sent)
    contact = call(
        contact_kernel, f32(3, ROWS, NK),
        arrived, sent, first, face_row, face_lane, next_normals, slot_of, at_slaves, gaps, slaves,
        scratch=[(2, SLOTS, PATCH), (6, PAIRS, PATCH)],
    )
    block = (3, NI, NJ, NK)
    u, v = call(
        finish_kernel, (plain(*block), plain(*block)),
        near, other, moduli, contact.reshape(block), u.reshape(block), v.reshape(block),
        mass.reshape(NI, NJ, NK),
    )
    return u.reshape(displacement.shape), v.reshape(velocity.shape)


def solution(mesh):
    nodal = P("len", "wid", "lay")
    vector = P(None, "len", "wid", "lay")
    in_specs = (
        vector, vector, nodal, nodal, nodal,
        P("len", "wid", "lay", None, None),
        P("len", "wid", "lay", None, None),
        P("len", "wid", "lay", None, None),
        P("len", "wid", "lay", None, None),
        P("len", "wid", "lay", None),
        P("len", "wid", "lay", None, None),
    )
    return jax.shard_map(
        program, mesh=mesh, in_specs=in_specs, out_specs=(vector, vector), check_vma=False
    )
```
